256 devices in a mesh: mem: 32 (over y, z), lev: 8 (over x, core).
Axes of the slice: x: 4, y: 4, z: 8, core: 2. Of those that a mesh axis runs over, the one named last changes fastest.
Arguments:
- prior_ensemble_stack: float32 [64, 40, 64, 512], P('mem', 'lev'), may hold values from -6 to 6
- vertical_cfl_ratio: float32 [40, 64, 512], P('lev'), may hold values from -0.35 to 0.35
- horizontal_cfl_ratio: float32 [40, 64, 512], P('lev'), may hold values from -0.35 to 0.35
- spreading_coefficient: float32 [40], P('lev'), may hold values from 0.02 to 0.2
- obs_cells: int32 [2, 16], replicated, may hold values from 0 to 32767
- obs_slabs: int32 [2, 16], replicated, may hold values from 0 to 39
- obs_values: float32 [2, 16], replicated, may hold values from -6 to 6
- obs_error: float32 [2, 16], replicated, may hold values from 0.25 to 2
Outputs:
- analysis: float32 [64, 40, 64, 512], P('mem', 'lev')
The draws below stay inside these ranges and needn't reach their ends.
All inputs are finite; a program needn't handle non-finite values.
Results may differ from the reference program's by a relative error of at most 0.0001.
Values sent between devices are 32-bit elements; how exact they have to be, the bound alone decides.
A program may use at most 256 MiB of HBM per device.

```python
import math
import jax
import jax.numpy as jnp
from jax import lax

NY = 64
NX = 512
STEPS = 2
BATCHES = 2
OBS = 16
MEMBERS = 64
SLABS = 40
LOC_HALF = 64


def place_ends(array, own_key, smallest, high):
    index_at = [jax.random.randint(jax.random.fold_in(own_key, axis), (), 0, length) for axis, length in enumerate(array.shape)]
    widest = array.shape.index(max(array.shape))
    beside = index_at[:widest] + [(index_at[widest] + 1) % array.shape[widest]] + index_at[widest + 1:]
    return array.at[tuple(index_at)].set(smallest).at[tuple(beside)].set(high)


def block_scale(stream_key, shape, cuts, low, high):
    factor_of = 1.0
    for axis_at, blocks in cuts:
        heights = jax.random.uniform(jax.random.fold_in(jax.random.fold_in(stream_key, 6), axis_at), (blocks,), jnp.float32, low / len(cuts), high / len(cuts))
        factor_of = factor_of * jnp.repeat(jnp.exp(heights), shape[axis_at] // blocks).reshape((-1,) + (1,) * (len(shape) - 1 - axis_at))
    return factor_of


def centred(key, shape, scale, limit, pieces=(), kind=jnp.bfloat16):
    entries = scale * jax.random.normal(key, shape, jnp.float32)
    if pieces:
        entries = entries * block_scale(key, shape, pieces, -0.22, 0.18)
    return jnp.clip(entries, -limit, limit).astype(kind)


def setup_inputs(seed: int = 0) -> dict:
    splits = jax.random.split(jax.random.key(seed), 9)
    return {
        "prior_ensemble_stack": centred(splits[0], (MEMBERS, SLABS, NY, NX), 1.0, 6.0, ((0, 32), (1, 8)), jnp.float32),
        "vertical_cfl_ratio": jnp.clip(jax.random.uniform(splits[1], (SLABS, NY, NX), jnp.float32, -0.35, 0.35) * block_scale(splits[1], (SLABS, NY, NX), ((0, 8),), -0.4, 0.0), -0.35, 0.35),
        "horizontal_cfl_ratio": jnp.clip(jax.random.uniform(splits[2], (SLABS, NY, NX), jnp.float32, -0.35, 0.35) * block_scale(splits[2], (SLABS, NY, NX), ((0, 8),), -0.4, 0.0), -0.35, 0.35),
        "spreading_coefficient": jnp.clip(jnp.exp(math.log(0.2) - 2.3025851 * jax.random.uniform(splits[3], (SLABS,), jnp.float32) ** block_scale(splits[3], (SLABS,), ((0, 8),), -0.2, 0.2)), 0.02, 0.2),
        "obs_cells": place_ends(jax.random.randint(splits[4], (BATCHES, OBS), 0, NY * NX), jax.random.fold_in(splits[4], 1), 0, (NY * NX) - 1).astype(jnp.int32),
        "obs_slabs": place_ends(jax.random.randint(splits[5], (BATCHES, OBS), 0, SLABS), jax.random.fold_in(splits[5], 1), 0, SLABS - 1).astype(jnp.int32),
        "obs_values": centred(splits[6], (BATCHES, OBS), 1.5, 6.0, (), jnp.float32),
        "obs_error": jnp.clip(jnp.exp(jax.random.uniform(splits[7], (BATCHES, OBS), jnp.float32, math.log(0.25), math.log(2.0))), 0.25, 2.0),
    }


def predicted_model_vector(ensemble_gridded_values, vertical_cfl_ratio, horizontal_cfl_ratio, spreading_coefficient):
    diffuse = spreading_coefficient[:, None, None]
    for time_step in range(STEPS):
        widths = [(0, 0)] * (ensemble_gridded_values.ndim - 2) + [(1, 1), (1, 1)]
        padded = jnp.pad(ensemble_gridded_values, widths, mode='edge')
        east_cell = padded[..., 1:-1, 2:]
        west_cell = padded[..., 1:-1, :-2]
        north_cell = padded[..., 2:, 1:-1]
        south_cell = padded[..., :-2, 1:-1]
        ensemble_gridded_values = ensemble_gridded_values - 0.5 * vertical_cfl_ratio * (east_cell - west_cell) - 0.5 * horizontal_cfl_ratio * (north_cell - south_cell) + diffuse * (east_cell + west_cell + north_cell + south_cell - 4.0 * ensemble_gridded_values)
    return ensemble_gridded_values

def grid_distance(cells_a, cells_b):
    row_gap = (cells_a[:, None] // NX - cells_b[None, :] // NX).astype(jnp.float32)
    col_gap = (cells_a[:, None] % NX - cells_b[None, :] % NX).astype(jnp.float32)
    return jnp.sqrt(row_gap * row_gap + col_gap * col_gap)

def gaspari_taper(dist):
    scaled = dist / LOC_HALF
    inner_portion = (((-0.25 * scaled + 0.5) * scaled + 0.625) * scaled - 5.0 / 3.0) * scaled * scaled + 1.0
    safe_ratio = jnp.maximum(scaled, 1.0)
    outer_portion = ((((scaled / 12.0 - 0.5) * scaled + 0.625) * scaled + 5.0 / 3.0) * scaled - 5.0) * scaled + 4.0 - 2.0 / (3.0 * safe_ratio)
    return jnp.where(scaled <= 1.0, inner_portion, jnp.where(scaled < 2.0, outer_portion, 0.0))

def obs_space(prior_rows, row_cells, first_row, obs_cell, obs_value, obs_var):
    member_count = prior_rows.shape[1]
    reach_table = gaspari_taper(grid_distance(row_cells, obs_cell))

    def advance_obs(current, position):
        own_row = lax.dynamic_index_in_dim(current, first_row + position, 0, False)
        row_mean = jnp.mean(own_row)
        anomaly = own_row - row_mean
        spread = jnp.sum(anomaly * anomaly) / (member_count - 1) + 1e-06
        error_var = lax.dynamic_index_in_dim(obs_var, position, 0, False)
        seen_value = lax.dynamic_index_in_dim(obs_value, position, 0, False)
        shrink = jnp.sqrt(error_var / (spread + error_var))
        increment = (row_mean * error_var + seen_value * spread) / (spread + error_var) - row_mean + (shrink - 1.0) * anomaly
        centered = current - lax.optimization_barrier(jnp.mean(current, axis=1, keepdims=True))
        slopes = jnp.dot(centered, anomaly, precision=lax.Precision.HIGHEST) / ((member_count - 1) * spread)
        weight = lax.dynamic_index_in_dim(reach_table, position, 1, False)
        current = current + (weight * slopes)[:, None] * increment[None, :]
        return (current, (anomaly, spread, increment))
    positions = jnp.arange(obs_cell.shape[0], dtype=jnp.int32)
    prior_rows, obs_plan = lax.scan(advance_obs, prior_rows, positions)
    return (obs_plan, prior_rows)

def settle(state_rows, obs_plan, cell_loc):
    prior_anoms, spreads, increments = obs_plan
    member_count = state_rows.shape[0]
    centered = state_rows - lax.optimization_barrier(jnp.mean(state_rows, axis=0, keepdims=True))
    cross_cov = jnp.einsum('km,msc->ksc', prior_anoms, centered, precision=lax.Precision.HIGHEST) / (member_count - 1)
    incr_anom = increments - lax.optimization_barrier(jnp.mean(increments, axis=1, keepdims=True))
    incr_link = jnp.dot(incr_anom, prior_anoms.T, precision=lax.Precision.HIGHEST) / (member_count - 1)

    def solve_step(weights, position):
        column = lax.dynamic_index_in_dim(incr_link, position, 1, False)
        summed_total = lax.dynamic_index_in_dim(cross_cov, position, 0, False) + jnp.einsum('j,jsc->sc', column, weights, precision=lax.Precision.HIGHEST)
        taper_row = lax.dynamic_index_in_dim(cell_loc, position, 0, False)
        update_row = taper_row[None, :] * summed_total / lax.dynamic_index_in_dim(spreads, position, 0, False)
        return (lax.dynamic_update_index_in_dim(weights, update_row, position, 0), None)
    positions = jnp.arange(cross_cov.shape[0], dtype=jnp.int32)
    weights, unused = lax.scan(solve_step, jnp.zeros_like(cross_cov), positions)
    return state_rows + jnp.einsum('km,ksc->msc', increments, weights, precision=lax.Precision.HIGHEST)

def reference(prior_ensemble_stack, vertical_cfl_ratio, horizontal_cfl_ratio, spreading_coefficient, obs_cells, obs_slabs, obs_values, obs_error):

    def advance_member(lone_realization_vector):
        return predicted_model_vector(lone_realization_vector, vertical_cfl_ratio, horizontal_cfl_ratio, spreading_coefficient)
    ensemble_gridded_values = lax.map(advance_member, prior_ensemble_stack)
    member_count = prior_ensemble_stack.shape[0]
    state_rows = ensemble_gridded_values.reshape(member_count, SLABS, NY * NX)
    grid_cells = jnp.arange(NY * NX, dtype=jnp.int32)
    for batch_no in range(BATCHES):
        prior_rows = state_rows[:, obs_slabs[batch_no], obs_cells[batch_no]].T
        obs_plan, carried = obs_space(prior_rows, obs_cells[batch_no], 0, obs_cells[batch_no], obs_values[batch_no], obs_error[batch_no])
        cell_loc = gaspari_taper(grid_distance(obs_cells[batch_no], grid_cells))
        state_rows = settle(state_rows, obs_plan, cell_loc)
    return state_rows.reshape(prior_ensemble_stack.shape)
```

```python
import functools

import jax
import jax.numpy as jnp
from jax import lax
from jax.experimental import pallas as pl
from jax.experimental.pallas import tpu as pltpu
from jax.sharding import PartitionSpec as P

NX = 512
STEPS = 2
LOC_HALF = 64
MESH = pl.DeviceIdType.MESH
ROWS, LANES = 8, 128
EARLY = 2


def taper(dist):
    scaled = dist * (1.0 / LOC_HALF)
    inner = (
        ((-0.25 * scaled + 0.5) * scaled + 0.625) * scaled - 5.0 / 3.0
    ) * scaled * scaled + 1.0
    safe = jnp.maximum(scaled, 1.0)
    outer = (
        ((((scaled * (1.0 / 12.0) - 0.5) * scaled + 0.625) * scaled + 5.0 / 3.0) * scaled - 5.0)
        * scaled
        + 4.0
        - 2.0 / (3.0 * safe)
    )
    return jnp.where(scaled <= 1.0, inner, jnp.where(scaled < 2.0, outer, 0.0))


def kernel(
    n_mem,
    n_lev,
    prior,
    vert,
    horz,
    diff,
    cells,
    slabs,
    vals,
    errs,
    out,
    pin,
    vin,
    hin,
    coef,
    field,
    blocks,
    got_lev,
    got_mem,
    msg,
    picked,
    square,
    anom,
    mean,
    obs_loc,
    place,
    plan,
    table,
    cell_loc,
    push,
    in_sem,
    lev_send,
    lev_recv,
    mem_send,
    mem_recv,
    out_send,
    out_recv,
    back_send,
    back_recv,
    plan_sem,
    own_sem,
):
    mem_dev, n_slab, grid_rows, grid_cols = prior.shape
    n_batch, n_per = cells.shape
    n_obs = n_batch * n_per
    members = mem_dev * n_mem
    half = LANES // mem_dev
    tiles_across = grid_cols // LANES
    me = lax.axis_index("mem")
    lev = lax.axis_index("lev")
    tile_row, tile_col = me // tiles_across, me % tiles_across

    def tile_of(ref, lead, d):
        r = pl.multiple_of((d // tiles_across) * ROWS, ROWS)
        c = pl.multiple_of((d % tiles_across) * LANES, LANES)
        return ref.at[lead + (pl.ds(r, ROWS), pl.ds(c, LANES))]

    def fetch(s):
        return (
            pltpu.make_async_copy(prior.at[:, s], pin.at[s], in_sem.at[0, s]),
            pltpu.make_async_copy(vert.at[s], vin.at[s], in_sem.at[1, s]),
            pltpu.make_async_copy(horz.at[s], hin.at[s], in_sem.at[2, s]),
        )

    @pl.loop(0, n_slab)
    def _(s):
        for copy in fetch(s):
            copy.start()

    barrier = pltpu.get_barrier_semaphore()

    @pl.loop(1, n_mem)
    def _(i):
        pl.semaphore_signal(
            barrier, inc=1, device_id={"mem": lax.rem(me + i, n_mem)}, device_id_type=MESH
        )

    @pl.loop(1, n_lev)
    def _(i):
        pl.semaphore_signal(
            barrier, inc=1, device_id={"lev": lax.rem(lev + i, n_lev)}, device_id_type=MESH
        )

    col = lax.broadcasted_iota(jnp.int32, (grid_rows, grid_cols), 1)
    row = lax.broadcasted_iota(jnp.int32, (grid_rows, grid_cols), 0)

    def forecast(s):
        for copy in fetch(s):
            copy.wait()
        d = diff[s]
        v = 0.5 * vin[s]
        h = 0.5 * hin[s]
        coef[0] = d - v
        coef[1] = d + v
        coef[2] = d - h
        coef[3] = d + h
        centre = 1.0 - 4.0 * d

        @pl.loop(0, mem_dev)
        def _(p):
            f = pin[s, p]
            for _step in range(STEPS):
                east = jnp.where(col == grid_cols - 1, f, pltpu.roll(f, grid_cols - 1, 1))
                west = jnp.where(col == 0, f, pltpu.roll(f, 1, 1))
                north = jnp.where(row == grid_rows - 1, f, pltpu.roll(f, grid_rows - 1, 0))
                south = jnp.where(row == 0, f, pltpu.roll(f, 1, 0))
                f = (
                    centre * f
                    + (coef[0] * east + coef[1] * west)
                    + (coef[2] * north + coef[3] * south)
                )
            field[s, p] = f

    def send_blocks(s):
        for p in range(mem_dev):
            blocks[s, me, p] = field[
                s,
                p,
                pl.ds(pl.multiple_of(tile_row * ROWS, ROWS), ROWS),
                pl.ds(pl.multiple_of(tile_col * LANES, LANES), LANES),
            ]

        @pl.loop(1, n_mem)
        def _(i):
            d = lax.rem(me + i, n_mem)
            pltpu.make_async_remote_copy(
                src_ref=tile_of(field, (s, slice(None)), d),
                dst_ref=blocks.at[s, me],
                send_sem=out_send.at[s],
                recv_sem=out_recv.at[s],
                device_id={"mem": d},
                device_id_type=MESH,
            ).start()

    forecast(0)
    pl.semaphore_wait(barrier, n_mem - 1 + n_lev - 1)
    send_blocks(0)

    @pl.loop(1, EARLY)
    def _(s):
        forecast(s)
        send_blocks(s)

    @pl.loop(EARLY, n_slab)
    def _(s):
        forecast(s)

    lane512 = lax.broadcasted_iota(jnp.int32, (1, grid_cols), 1)

    @pl.loop(0, n_obs)
    def _(k):
        b, q = k // n_per, lax.rem(k, n_per)
        cell = cells[b, q]
        at_row, at_col = lax.shift_right_logical(cell, 9), jnp.bitwise_and(cell, NX - 1)
        off = slabs[b, q] - lev * n_slab
        inside = jnp.logical_and(off >= 0, off < n_slab)
        wanted = jnp.where(inside, at_col, -1)
        near = jnp.clip(off, 0, n_slab - 1)
        for p in range(mem_dev):
            line = field[near, p, pl.ds(at_row, 1), :]
            line = jnp.where(lane512 == wanted, line, 0.0)
            total = line[:, :LANES]
            for t in range(1, tiles_across):
                total = total + line[:, t * LANES : (t + 1) * LANES]
            picked[p, pl.ds(k, 1), :] = total
        place[0, pl.ds(k, 1), :] = jnp.full((1, LANES), at_row.astype(jnp.float32))
        place[1, pl.ds(k, 1), :] = jnp.full((1, LANES), at_col.astype(jnp.float32))

    sub32 = lax.broadcasted_iota(jnp.int32, (n_obs, LANES), 0)
    lane32 = lax.broadcasted_iota(jnp.int32, (n_obs, LANES), 1)
    share = jnp.zeros((1, LANES), jnp.float32)
    for p in range(mem_dev):
        column = jnp.sum(picked[p], axis=1, keepdims=True)
        share = share + jnp.sum(
            jnp.where(lane32 == sub32 + p * half, column, 0.0), axis=0, keepdims=True
        )
    msg[0] = share
    got_lev[lev] = share

    @pl.loop(1, n_lev)
    def _(i):
        pltpu.make_async_remote_copy(
            src_ref=msg.at[0],
            dst_ref=got_lev.at[lev],
            send_sem=lev_send,
            recv_sem=lev_recv,
            device_id={"lev": lax.rem(lev + i, n_lev)},
            device_id_type=MESH,
        ).start()

    cell_row = (
        tile_row * ROWS + lax.broadcasted_iota(jnp.int32, (ROWS, LANES), 0)
    ).astype(jnp.float32)
    cell_col = (
        tile_col * LANES + lax.broadcasted_iota(jnp.int32, (ROWS, LANES), 1)
    ).astype(jnp.float32)

    def lev_rows(copies):
        return got_lev.at[pl.ds(0, copies)]

    pltpu.make_async_copy(lev_rows(n_lev - 1), lev_rows(n_lev - 1), lev_recv).wait()
    total = got_lev[0]
    for i in range(1, n_lev):
        total = total + got_lev[i]
    msg[1] = total
    got_mem[me] = total

    @pl.loop(1, n_mem)
    def _(i):
        pltpu.make_async_remote_copy(
            src_ref=msg.at[1],
            dst_ref=got_mem.at[me],
            send_sem=mem_send,
            recv_sem=mem_recv,
            device_id={"mem": lax.rem(me + i, n_mem)},
            device_id_type=MESH,
        ).start()

    @pl.loop(EARLY, n_slab)
    def _(s):
        send_blocks(s)

    @pl.loop(0, n_obs)
    def _(k):
        b, q = k // n_per, lax.rem(k, n_per)
        cell = cells[b, q]
        r = lax.shift_right_logical(cell, 9).astype(jnp.float32)
        c = jnp.bitwise_and(cell, NX - 1).astype(jnp.float32)
        dr, dc = place[0] - r, place[1] - c
        obs_loc[k] = taper(jnp.sqrt(dr * dr + dc * dc))
        dr, dc = cell_row - r, cell_col - c
        cell_loc[k] = taper(jnp.sqrt(dr * dr + dc * dc))

    square[...] = jnp.zeros_like(square)
    pltpu.make_async_copy(
        got_mem.at[pl.ds(0, n_mem - 1)], got_mem.at[pl.ds(0, n_mem - 1)], mem_recv
    ).wait()

    @pl.loop(0, n_mem)
    def _(i):
        square[pl.ds(i, 1), :] = got_mem[i]

    turned = square[...].T
    rows = turned[:n_obs]
    for p in range(1, mem_dev):
        rows = rows + pltpu.roll(turned[p * half : p * half + n_obs], p * half, 1)
    rows_mean = jnp.sum(rows, axis=1, keepdims=True) * (1.0 / members)
    used = lax.rem(lane32, half) < n_mem
    anom[...] = jnp.where(used, rows - rows_mean, 0.0)
    mean[...] = jnp.broadcast_to(rows_mean, (n_obs, LANES))
    lane1 = lax.broadcasted_iota(jnp.int32, (1, LANES), 1)

    @pl.loop(0, n_obs)
    def _(k):
        b, q = k // n_per, lax.rem(k, n_per)
        r, o = errs[b, q], vals[b, q]
        a = anom[pl.ds(k, 1), :]
        m = mean[pl.ds(k, 1), :]
        every = anom[...]
        g = jnp.sum(every * a, axis=1, keepdims=True)
        v = jnp.sum(a * a, axis=1, keepdims=True) * (1.0 / (members - 1)) + 1e-06
        v = jnp.broadcast_to(v, (1, LANES))
        inv = 1.0 / (v + r)
        less = jnp.sqrt(r * inv) - 1.0
        move = (m * r + o * v) * inv - m
        gain = 1.0 / ((members - 1) * v)
        c = obs_loc[k] * g * gain
        anom[...] = every + (c * less) * a
        mean[...] = mean[...] + c * move
        plan[pl.ds(k, 1), :] = a
        plan[pl.ds(2 * n_obs + k, 1), :] = jnp.where(
            lane1 == 0, less, jnp.where(lane1 == 1, move, gain)
        )

    y = plan[:n_obs]
    link = lax.dot_general(
        y,
        y,
        (((1,), (1,)), ((), ())),
        precision=lax.Precision.HIGHEST,
        preferred_element_type=jnp.float32,
    )
    plan[n_obs : 2 * n_obs, :n_obs] = link
    to_table = pltpu.make_async_copy(plan, table, plan_sem)
    to_table.start()
    to_table.wait()

    width = 8
    spread = width // mem_dev

    @pl.loop(0, n_slab)
    def _(s):
        pltpu.make_async_copy(
            blocks.at[s, pl.ds(0, n_mem - 1)], blocks.at[s, pl.ds(0, n_mem - 1)], out_recv.at[s]
        ).wait()

        def add_up(t, acc):
            for u in range(spread):
                for p in range(mem_dev):
                    acc = acc + blocks[s, t * spread + u, p]
            return acc

        zero = jnp.zeros((ROWS, LANES), jnp.float32)
        centre = lax.fori_loop(0, n_mem // spread, add_up, zero) * (1.0 / members)

        def solve(kb, base):
            k0 = kb * width

            def dots(t, acc):
                acc = list(acc)
                for u in range(spread):
                    i = t * spread + u
                    for p in range(mem_dev):
                        x = blocks[s, i, p] - centre
                        for e in range(width):
                            acc[e] = acc[e] + table[k0 + e, p * half + i] * x
                return tuple(acc)

            def links(jb, acc):
                acc = list(acc)
                for f in range(width):
                    j = jb * width + f
                    x = push[j]
                    for e in range(width):
                        acc[e] = acc[e] + table[n_obs + k0 + e, j] * x
                return tuple(acc)

            acc = lax.fori_loop(0, n_mem // spread, dots, (zero,) * width)
            acc = list(lax.fori_loop(0, kb, links, acc))
            for e in range(width):
                k = k0 + e
                w = (cell_loc[k] * table[2 * n_obs + k, 2]) * acc[e]
                pushed = table[2 * n_obs + k, 0] * w
                base = base + table[2 * n_obs + k, 1] * w
                push[k] = pushed
                for f in range(e + 1, width):
                    acc[f] = acc[f] + table[n_obs + k0 + f, k] * pushed
            return base

        base = lax.fori_loop(0, n_obs // width, solve, zero)

        @pl.loop(0, n_mem // spread)
        def _(t):
            own = [lax.rem(me + t * spread + u, n_mem) for u in range(spread)]
            at = [(i, p) for i in own for p in range(mem_dev)]

            def apply(kb, acc):
                acc = list(acc)
                for e in range(width):
                    k = kb * width + e
                    x = push[k]
                    for g, (i, p) in enumerate(at):
                        acc[g] = acc[g] + table[k, p * half + i] * x
                return tuple(acc)

            acc = lax.fori_loop(
                0, n_obs // width, apply, tuple(blocks[s, i, p] + base for i, p in at)
            )
            for g, (i, p) in enumerate(at):
                blocks[s, i, p] = acc[g]
            for u in range(spread):

                @pl.when(t * spread + u > 0)
                def _():
                    pltpu.make_async_remote_copy(
                        src_ref=blocks.at[s, own[u]],
                        dst_ref=tile_of(out, (slice(None), s), me),
                        send_sem=back_send,
                        recv_sem=back_recv,
                        device_id={"mem": own[u]},
                        device_id_type=MESH,
                    ).start()

    def own_copy(s):
        return pltpu.make_async_copy(
            blocks.at[s, me], tile_of(out, (slice(None), s), me), own_sem.at[s]
        )

    @pl.loop(0, n_slab)
    def _(s):
        own_copy(s).start()

    others = blocks.at[:, pl.ds(0, n_mem - 1)]

    @pl.loop(0, n_slab)
    def _(s):
        sent = blocks.at[s, pl.ds(0, n_mem - 1)]
        pltpu.make_async_copy(sent, sent, out_send.at[s]).wait()
        own_copy(s).wait()

    pltpu.make_async_copy(lev_rows(n_lev - 1), lev_rows(n_lev - 1), lev_send).wait()
    pltpu.make_async_copy(
        got_mem.at[pl.ds(0, n_mem - 1)], got_mem.at[pl.ds(0, n_mem - 1)], mem_send
    ).wait()
    pltpu.make_async_copy(others, others, back_send).wait()
    pltpu.make_async_copy(others, others, back_recv).wait()


def body(prior, vert, horz, diff, cells, slabs, vals, errs):
    n_mem, n_lev = lax.axis_size("mem"), lax.axis_size("lev")
    mem_dev, n_slab, grid_rows, grid_cols = prior.shape
    n_obs = cells.size
    f32 = jnp.float32
    whole = pl.BlockSpec(memory_space=pl.ANY)
    scalars = pl.BlockSpec(memory_space=pltpu.SMEM)
    dma = pltpu.SemaphoreType.DMA
    return pl.pallas_call(
        functools.partial(kernel, n_mem, n_lev),
        out_shape=jax.ShapeDtypeStruct(prior.shape, prior.dtype),
        in_specs=[whole] * 3 + [scalars] * 5,
        out_specs=whole,
        scratch_shapes=[
            pltpu.VMEM((n_slab, mem_dev, grid_rows, grid_cols), f32),
            pltpu.VMEM((n_slab, grid_rows, grid_cols), f32),
            pltpu.VMEM((n_slab, grid_rows, grid_cols), f32),
            pltpu.VMEM((4, grid_rows, grid_cols), f32),
            pltpu.VMEM((n_slab, mem_dev, grid_rows, grid_cols), f32),
            pltpu.VMEM((n_slab, n_mem, mem_dev, ROWS, LANES), f32),
            pltpu.VMEM((n_lev, 1, LANES), f32),
            pltpu.VMEM((n_mem, 1, LANES), f32),
            pltpu.VMEM((2, 1, LANES), f32),
            pltpu.VMEM((mem_dev, n_obs, LANES), f32),
            pltpu.VMEM((LANES, LANES), f32),
            pltpu.VMEM((n_obs, LANES), f32),
            pltpu.VMEM((n_obs, LANES), f32),
            pltpu.VMEM((n_obs, n_obs, LANES), f32),
            pltpu.VMEM((2, n_obs, LANES), f32),
            pltpu.VMEM((3 * n_obs, LANES), f32),
            pltpu.SMEM((3 * n_obs, LANES), f32),
            pltpu.VMEM((n_obs, ROWS, LANES), f32),
            pltpu.VMEM((n_obs, ROWS, LANES), f32),
            dma((3, n_slab)),
            dma,
            dma,
            dma,
            dma,
            dma((n_slab,)),
            dma((n_slab,)),
            dma,
            dma,
            dma,
            dma((n_slab,)),
        ],
        compiler_params=pltpu.CompilerParams(
            collective_id=0, has_side_effects=True, vmem_limit_bytes=40 << 20
        ),
        name="filter_cycle",
    )(prior, vert, horz, diff, cells, slabs, vals, errs)


def solution(mesh):
    in_specs = (
        P("mem", "lev", None, None),
        P("lev", None, None),
        P("lev", None, None),
        P("lev"),
        P(),
        P(),
        P(),
        P(),
    )
    out_specs = P("mem", "lev", None, None)
    return jax.shard_map(body, mesh=mesh, in_specs=in_specs, out_specs=out_specs, check_vma=False)
```

```python
import functools

import jax
import jax.numpy as jnp
from jax import lax
from jax.experimental import pallas as pl
from jax.experimental.pallas import tpu as pltpu
from jax.sharding import PartitionSpec as P

NX = 512
STEPS = 2
LOC_HALF = 64
MESH = pl.DeviceIdType.MESH
ROWS, LANES = 8, 128
EARLY = 2


def taper(dist):
    scaled = dist * (1.0 / LOC_HALF)
    inner = (
        ((-0.25 * scaled + 0.5) * scaled + 0.625) * scaled - 5.0 / 3.0
    ) * scaled * scaled + 1.0
    safe = jnp.maximum(scaled, 1.0)
    outer = (
        ((((scaled * (1.0 / 12.0) - 0.5) * scaled + 0.625) * scaled + 5.0 / 3.0) * scaled - 5.0)
        * scaled
        + 4.0
        - 2.0 / (3.0 * safe)
    )
    return jnp.where(scaled <= 1.0, inner, jnp.where(scaled < 2.0, outer, 0.0))


def kernel(
    n_mem,
    n_lev,
    prior,
    vert,
    horz,
    diff_in,
    cells_in,
    slabs_in,
    vals_in,
    errs_in,
    out,
    diff,
    cells,
    slabs,
    vals,
    errs,
    pin,
    vin,
    hin,
    coef,
    field,
    blocks,
    got_lev,
    got_mem,
    msg,
    picked,
    square,
    anom,
    mean,
    obs_loc,
    place,
    plan,
    table,
    cell_loc,
    ys,
    wide,
    tall,
    spread_in,
    spread_out,
    centred,
    cross,
    push,
    in_sem,
    obs_sem,
    lev_send,
    lev_recv,
    mem_send,
    mem_recv,
    out_send,
    out_recv,
    back_send,
    back_recv,
    plan_sem,
    own_sem,
):
    mem_dev, n_slab, grid_rows, grid_cols = prior.shape
    n_batch, n_per = cells.shape
    n_obs = n_batch * n_per
    members = mem_dev * n_mem
    half = LANES // mem_dev
    tiles_across = grid_cols // LANES
    me = lax.axis_index("mem")
    lev = lax.axis_index("lev")
    tile_row, tile_col = me // tiles_across, me % tiles_across

    def tile_of(ref, lead, d):
        r = pl.multiple_of((d // tiles_across) * ROWS, ROWS)
        c = pl.multiple_of((d % tiles_across) * LANES, LANES)
        return ref.at[lead + (pl.ds(r, ROWS), pl.ds(c, LANES))]

    def fetch(s):
        return (
            pltpu.make_async_copy(prior.at[:, s], pin.at[s], in_sem.at[0, s]),
            pltpu.make_async_copy(vert.at[s], vin.at[s], in_sem.at[1, s]),
            pltpu.make_async_copy(horz.at[s], hin.at[s], in_sem.at[2, s]),
        )

    small = [
        pltpu.make_async_copy(a, b, obs_sem.at[i])
        for i, (a, b) in enumerate(
            (
                (diff_in, diff),
                (cells_in, cells),
                (slabs_in, slabs),
                (vals_in, vals),
                (errs_in, errs),
            )
        )
    ]
    for copy in small:
        copy.start()

    @pl.loop(0, n_slab)
    def _(s):
        for copy in fetch(s):
            copy.start()

    barrier = pltpu.get_barrier_semaphore()

    @pl.loop(1, n_mem)
    def _(i):
        pl.semaphore_signal(
            barrier, inc=1, device_id={"mem": lax.rem(me + i, n_mem)}, device_id_type=MESH
        )

    @pl.loop(1, n_lev)
    def _(i):
        pl.semaphore_signal(
            barrier, inc=1, device_id={"lev": lax.rem(lev + i, n_lev)}, device_id_type=MESH
        )

    col = lax.broadcasted_iota(jnp.int32, (grid_rows, grid_cols), 1)
    row = lax.broadcasted_iota(jnp.int32, (grid_rows, grid_cols), 0)

    def forecast(s):
        for copy in fetch(s):
            copy.wait()
        d = diff[s]
        v = 0.5 * vin[s]
        h = 0.5 * hin[s]
        coef[0] = d - v
        coef[1] = d + v
        coef[2] = d - h
        coef[3] = d + h
        centre = 1.0 - 4.0 * d

        @pl.loop(0, mem_dev)
        def _(p):
            f = pin[s, p]
            for _step in range(STEPS):
                east = jnp.where(col == grid_cols - 1, f, pltpu.roll(f, grid_cols - 1, 1))
                west = jnp.where(col == 0, f, pltpu.roll(f, 1, 1))
                north = jnp.where(row == grid_rows - 1, f, pltpu.roll(f, grid_rows - 1, 0))
                south = jnp.where(row == 0, f, pltpu.roll(f, 1, 0))
                f = (
                    centre * f
                    + (coef[0] * east + coef[1] * west)
                    + (coef[2] * north + coef[3] * south)
                )
            field[s, p] = f

    def send_blocks(s):
        for p in range(mem_dev):
            blocks[s, me, p] = field[
                s,
                p,
                pl.ds(pl.multiple_of(tile_row * ROWS, ROWS), ROWS),
                pl.ds(pl.multiple_of(tile_col * LANES, LANES), LANES),
            ]

        @pl.loop(1, n_mem)
        def _(i):
            d = lax.rem(me + i, n_mem)
            pltpu.make_async_remote_copy(
                src_ref=tile_of(field, (s, slice(None)), d),
                dst_ref=blocks.at[s, me],
                send_sem=out_send.at[s],
                recv_sem=out_recv.at[s],
                device_id={"mem": d},
                device_id_type=MESH,
            ).start()

    for copy in small:
        copy.wait()
    forecast(0)
    pl.semaphore_wait(barrier, n_mem - 1 + n_lev - 1)
    send_blocks(0)

    @pl.loop(1, EARLY)
    def _(s):
        forecast(s)
        send_blocks(s)

    @pl.loop(EARLY, n_slab)
    def _(s):
        forecast(s)

    lane512 = lax.broadcasted_iota(jnp.int32, (1, grid_cols), 1)

    @pl.loop(0, n_obs)
    def _(k):
        b, q = k // n_per, lax.rem(k, n_per)
        cell = cells[b, q]
        at_row, at_col = lax.shift_right_logical(cell, 9), jnp.bitwise_and(cell, NX - 1)
        off = slabs[b, q] - lev * n_slab
        inside = jnp.logical_and(off >= 0, off < n_slab)
        wanted = jnp.where(inside, at_col, -1)
        near = jnp.clip(off, 0, n_slab - 1)
        for p in range(mem_dev):
            line = field[near, p, pl.ds(at_row, 1), :]
            line = jnp.where(lane512 == wanted, line, 0.0)
            total = line[:, :LANES]
            for t in range(1, tiles_across):
                total = total + line[:, t * LANES : (t + 1) * LANES]
            picked[p, pl.ds(k, 1), :] = total
        place[0, pl.ds(k, 1), :] = jnp.full((1, LANES), at_row.astype(jnp.float32))
        place[1, pl.ds(k, 1), :] = jnp.full((1, LANES), at_col.astype(jnp.float32))

    sub32 = lax.broadcasted_iota(jnp.int32, (n_obs, LANES), 0)
    lane32 = lax.broadcasted_iota(jnp.int32, (n_obs, LANES), 1)
    share = jnp.zeros((1, LANES), jnp.float32)
    for p in range(mem_dev):
        column = jnp.sum(picked[p], axis=1, keepdims=True)
        share = share + jnp.sum(
            jnp.where(lane32 == sub32 + p * half, column, 0.0), axis=0, keepdims=True
        )
    msg[0] = share
    got_lev[lev] = share

    @pl.loop(1, n_lev)
    def _(i):
        pltpu.make_async_remote_copy(
            src_ref=msg.at[0],
            dst_ref=got_lev.at[lev],
            send_sem=lev_send,
            recv_sem=lev_recv,
            device_id={"lev": lax.rem(lev + i, n_lev)},
            device_id_type=MESH,
        ).start()

    cell_row = (
        tile_row * ROWS + lax.broadcasted_iota(jnp.int32, (ROWS, LANES), 0)
    ).astype(jnp.float32)
    cell_col = (
        tile_col * LANES + lax.broadcasted_iota(jnp.int32, (ROWS, LANES), 1)
    ).astype(jnp.float32)

    def lev_rows(copies):
        return got_lev.at[pl.ds(0, copies)]

    pltpu.make_async_copy(lev_rows(n_lev - 1), lev_rows(n_lev - 1), lev_recv).wait()
    total = got_lev[0]
    for i in range(1, n_lev):
        total = total + got_lev[i]
    msg[1] = total
    got_mem[me] = total

    @pl.loop(1, n_mem)
    def _(i):
        pltpu.make_async_remote_copy(
            src_ref=msg.at[1],
            dst_ref=got_mem.at[me],
            send_sem=mem_send,
            recv_sem=mem_recv,
            device_id={"mem": lax.rem(me + i, n_mem)},
            device_id_type=MESH,
        ).start()

    @pl.loop(EARLY, n_slab)
    def _(s):
        send_blocks(s)

    @pl.loop(0, n_obs)
    def _(k):
        b, q = k // n_per, lax.rem(k, n_per)
        cell = cells[b, q]
        r = lax.shift_right_logical(cell, 9).astype(jnp.float32)
        c = jnp.bitwise_and(cell, NX - 1).astype(jnp.float32)
        dr, dc = place[0] - r, place[1] - c
        obs_loc[k] = taper(jnp.sqrt(dr * dr + dc * dc))
        dr, dc = cell_row - r, cell_col - c
        cell_loc[k] = taper(jnp.sqrt(dr * dr + dc * dc))

    square[...] = jnp.zeros_like(square)
    pltpu.make_async_copy(
        got_mem.at[pl.ds(0, n_mem - 1)], got_mem.at[pl.ds(0, n_mem - 1)], mem_recv
    ).wait()

    @pl.loop(0, n_mem)
    def _(i):
        square[pl.ds(i, 1), :] = got_mem[i]

    turned = square[...].T
    rows = turned[:n_obs]
    for p in range(1, mem_dev):
        rows = rows + pltpu.roll(turned[p * half : p * half + n_obs], p * half, 1)
    rows_mean = jnp.sum(rows, axis=1, keepdims=True) * (1.0 / members)
    used = lax.rem(lane32, half) < n_mem
    anom[...] = jnp.where(used, rows - rows_mean, 0.0)
    mean[...] = jnp.broadcast_to(rows_mean, (n_obs, LANES))
    lane1 = lax.broadcasted_iota(jnp.int32, (1, LANES), 1)

    @pl.loop(0, n_obs)
    def _(k):
        b, q = k // n_per, lax.rem(k, n_per)
        r, o = errs[b, q], vals[b, q]
        a = anom[pl.ds(k, 1), :]
        m = mean[pl.ds(k, 1), :]
        every = anom[...]
        g = jnp.sum(every * a, axis=1, keepdims=True)
        v = jnp.sum(a * a, axis=1, keepdims=True) * (1.0 / (members - 1)) + 1e-06
        v = jnp.broadcast_to(v, (1, LANES))
        inv = 1.0 / (v + r)
        less = jnp.sqrt(r * inv) - 1.0
        move = (m * r + o * v) * inv - m
        gain = 1.0 / ((members - 1) * v)
        c = obs_loc[k] * g * gain
        anom[...] = every + (c * less) * a
        mean[...] = mean[...] + c * move
        ys[pl.ds(k, 1), :] = a
        plan[pl.ds(n_obs + k, 1), :] = jnp.where(
            lane1 == 0, less, jnp.where(lane1 == 1, move, gain)
        )

    def product(a, b, axis=0):
        return lax.dot_general(
            a,
            b,
            (((1,), (axis,)), ((), ())),
            precision=lax.Precision.HIGHEST,
            preferred_element_type=jnp.float32,
        )

    y = ys[...]
    plan[:n_obs, :n_obs] = product(y, y, 1)
    square[:n_obs, :] = y
    square[n_obs:, :] = jnp.zeros((LANES - n_obs, LANES), jnp.float32)
    turned = square[...].T
    at = lax.broadcasted_iota(jnp.int32, (LANES, members * ROWS), 1) // ROWS
    lane_of = lax.rem(at, mem_dev) * half + at // mem_dev
    pick_in = (lane_of == lax.broadcasted_iota(jnp.int32, (LANES, members * ROWS), 0)).astype(
        jnp.float32
    )
    wide[...] = product(y, pick_in)
    pick_out = (
        lax.broadcasted_iota(jnp.int32, (LANES, n_obs * ROWS), 1) // ROWS
        == lax.broadcasted_iota(jnp.int32, (LANES, n_obs * ROWS), 0)
    ).astype(jnp.float32)
    tall[...] = product(turned, pick_out)

    def same_row(n):
        shape = (ROWS, n * ROWS)
        return lax.rem(lax.broadcasted_iota(jnp.int32, shape, 1), ROWS) == (
            lax.broadcasted_iota(jnp.int32, shape, 0)
        )

    @pl.loop(0, n_obs)
    def _(k):
        spread_in[pl.ds(pl.multiple_of(k * ROWS, ROWS), ROWS), :] = jnp.where(
            same_row(members), wide[pl.ds(k, 1), :], 0.0
        )

    @pl.loop(0, n_mem)
    def _(i):
        for p in range(mem_dev):
            at = pl.multiple_of((i * mem_dev + p) * ROWS, ROWS)
            spread_out[pl.ds(at, ROWS), :] = jnp.where(
                same_row(n_obs), tall[pl.ds(p * half + i, 1), :], 0.0
            )

    to_table = pltpu.make_async_copy(plan, table, plan_sem)
    to_table.start()
    to_table.wait()

    width = 8

    @pl.loop(0, n_slab)
    def _(s):
        pltpu.make_async_copy(
            blocks.at[s, pl.ds(0, n_mem - 1)], blocks.at[s, pl.ds(0, n_mem - 1)], out_recv.at[s]
        ).wait()

        x = blocks[s].reshape(members, ROWS, LANES)
        centre = jnp.sum(x, axis=0) * (1.0 / members)
        centred[...] = (x - centre).reshape(members * ROWS, LANES)
        cross[...] = product(spread_in[...], centred[...]).reshape(n_obs, ROWS, LANES)

        def solve(kb, base):
            k0 = kb * width

            def links(jb, acc):
                acc = list(acc)
                for f in range(width):
                    j = jb * width + f
                    x = push[j]
                    for e in range(width):
                        acc[e] = acc[e] + table[k0 + e, j] * x
                return tuple(acc)

            acc = tuple(cross[k0 + e] for e in range(width))
            acc = list(lax.fori_loop(0, kb, links, acc))
            for e in range(width):
                k = k0 + e
                w = (cell_loc[k] * table[n_obs + k, 2]) * acc[e]
                pushed = table[n_obs + k, 0] * w
                base = base + table[n_obs + k, 1] * w
                push[k] = pushed
                for f in range(e + 1, width):
                    acc[f] = acc[f] + table[k0 + f, k] * pushed
            return base

        base = lax.fori_loop(0, n_obs // width, solve, jnp.zeros((ROWS, LANES), jnp.float32))
        moved = product(spread_out[...], push[...].reshape(n_obs * ROWS, LANES))
        moved = moved.reshape(members, ROWS, LANES) + base
        blocks[s] = blocks[s] + moved.reshape(n_mem, mem_dev, ROWS, LANES)

        @pl.loop(1, n_mem)
        def _(i):
            d = lax.rem(me + i, n_mem)
            pltpu.make_async_remote_copy(
                src_ref=blocks.at[s, d],
                dst_ref=tile_of(out, (slice(None), s), me),
                send_sem=back_send,
                recv_sem=back_recv,
                device_id={"mem": d},
                device_id_type=MESH,
            ).start()

    def own_copy(s):
        return pltpu.make_async_copy(
            blocks.at[s, me], tile_of(out, (slice(None), s), me), own_sem.at[s]
        )

    @pl.loop(0, n_slab)
    def _(s):
        own_copy(s).start()

    others = blocks.at[:, pl.ds(0, n_mem - 1)]

    @pl.loop(0, n_slab)
    def _(s):
        sent = blocks.at[s, pl.ds(0, n_mem - 1)]
        pltpu.make_async_copy(sent, sent, out_send.at[s]).wait()
        own_copy(s).wait()

    pltpu.make_async_copy(lev_rows(n_lev - 1), lev_rows(n_lev - 1), lev_send).wait()
    pltpu.make_async_copy(
        got_mem.at[pl.ds(0, n_mem - 1)], got_mem.at[pl.ds(0, n_mem - 1)], mem_send
    ).wait()
    pltpu.make_async_copy(others, others, back_send).wait()
    pltpu.make_async_copy(others, others, back_recv).wait()


def body(prior, vert, horz, diff, cells, slabs, vals, errs):
    n_mem, n_lev = lax.axis_size("mem"), lax.axis_size("lev")
    mem_dev, n_slab, grid_rows, grid_cols = prior.shape
    n_obs = cells.size
    members = mem_dev * n_mem
    f32 = jnp.float32
    whole = pl.BlockSpec(memory_space=pl.ANY)
    dma = pltpu.SemaphoreType.DMA
    return pl.pallas_call(
        functools.partial(kernel, n_mem, n_lev),
        out_shape=jax.ShapeDtypeStruct(prior.shape, prior.dtype),
        in_specs=[whole] * 8,
        out_specs=whole,
        scratch_shapes=[
            pltpu.SMEM(diff.shape, diff.dtype),
            pltpu.SMEM(cells.shape, cells.dtype),
            pltpu.SMEM(slabs.shape, slabs.dtype),
            pltpu.SMEM(vals.shape, vals.dtype),
            pltpu.SMEM(errs.shape, errs.dtype),
            pltpu.VMEM((n_slab, mem_dev, grid_rows, grid_cols), f32),
            pltpu.VMEM((n_slab, grid_rows, grid_cols), f32),
            pltpu.VMEM((n_slab, grid_rows, grid_cols), f32),
            pltpu.VMEM((4, grid_rows, grid_cols), f32),
            pltpu.VMEM((n_slab, mem_dev, grid_rows, grid_cols), f32),
            pltpu.VMEM((n_slab, n_mem, mem_dev, ROWS, LANES), f32),
            pltpu.VMEM((n_lev, 1, LANES), f32),
            pltpu.VMEM((n_mem, 1, LANES), f32),
            pltpu.VMEM((2, 1, LANES), f32),
            pltpu.VMEM((mem_dev, n_obs, LANES), f32),
            pltpu.VMEM((LANES, LANES), f32),
            pltpu.VMEM((n_obs, LANES), f32),
            pltpu.VMEM((n_obs, LANES), f32),
            pltpu.VMEM((n_obs, n_obs, LANES), f32),
            pltpu.VMEM((2, n_obs, LANES), f32),
            pltpu.VMEM((2 * n_obs, LANES), f32),
            pltpu.SMEM((2 * n_obs, LANES), f32),
            pltpu.VMEM((n_obs, ROWS, LANES), f32),
            pltpu.VMEM((n_obs, LANES), f32),
            pltpu.VMEM((n_obs, members * ROWS), f32),
            pltpu.VMEM((LANES, n_obs * ROWS), f32),
            pltpu.VMEM((n_obs * ROWS, members * ROWS), f32),
            pltpu.VMEM((members * ROWS, n_obs * ROWS), f32),
            pltpu.VMEM((members * ROWS, LANES), f32),
            pltpu.VMEM((n_obs, ROWS, LANES), f32),
            pltpu.VMEM((n_obs, ROWS, LANES), f32),
            dma((3, n_slab)),
            dma((5,)),
            dma,
            dma,
            dma,
            dma,
            dma((n_slab,)),
            dma((n_slab,)),
            dma,
            dma,
            dma,
            dma((n_slab,)),
        ],
        compiler_params=pltpu.CompilerParams(
            collective_id=0, has_side_effects=True, vmem_limit_bytes=62 << 20
        ),
        name="filter_cycle",
    )(prior, vert, horz, diff, cells, slabs, vals, errs)


def solution(mesh):
    in_specs = (
        P("mem", "lev", None, None),
        P("lev", None, None),
        P("lev", None, None),
        P("lev"),
        P(),
        P(),
        P(),
        P(),
    )
    out_specs = P("mem", "lev", None, None)
    return jax.shard_map(body, mesh=mesh, in_specs=in_specs, out_specs=out_specs, check_vma=False)
```

```python
import functools

import jax
import jax.numpy as jnp
from jax import lax
from jax.experimental import pallas as pl
from jax.experimental.pallas import tpu as pltpu
from jax.sharding import PartitionSpec as P

NX = 512
STEPS = 2
LOC_HALF = 64
MESH = pl.DeviceIdType.MESH
ROWS, LANES = 8, 128
RING = 8
MIDDLE = 2
EARLY = 1


def taper(dist):
    scaled = dist * (1.0 / LOC_HALF)
    inner = (
        ((-0.25 * scaled + 0.5) * scaled + 0.625) * scaled - 5.0 / 3.0
    ) * scaled * scaled + 1.0
    safe = jnp.maximum(scaled, 1.0)
    outer = (
        ((((scaled * (1.0 / 12.0) - 0.5) * scaled + 0.625) * scaled + 5.0 / 3.0) * scaled - 5.0)
        * scaled
        + 4.0
        - 2.0 / (3.0 * safe)
    )
    return jnp.where(scaled <= 1.0, inner, jnp.where(scaled < 2.0, outer, 0.0))


def kernel(
    n_mem,
    n_lev,
    prior,
    vert,
    horz,
    diff_in,
    cells_in,
    slabs_in,
    vals_in,
    errs_in,
    out,
    diff,
    cells,
    slabs,
    vals,
    errs,
    pin,
    vin,
    hin,
    coef,
    field,
    blocks,
    got_lev,
    got_mem,
    msg,
    picked,
    square,
    anom,
    mean,
    obs_loc,
    place,
    plan,
    table,
    cell_loc,
    ys,
    wide,
    tall,
    spread_in,
    spread_out,
    centred,
    cross,
    push,
    in_sem,
    obs_sem,
    lev_send,
    lev_recv,
    mem_send,
    mem_recv,
    out_send,
    out_recv,
    back_send,
    back_recv,
    plan_sem,
    own_sem,
):
    mem_dev, n_slab, grid_rows, grid_cols = prior.shape
    n_batch, n_per = cells.shape
    n_obs = n_batch * n_per
    members = mem_dev * n_mem
    half = LANES // mem_dev
    tiles_across = grid_cols // LANES
    me = lax.axis_index("mem")
    lev = lax.axis_index("lev")
    tile_row, tile_col = me // tiles_across, me % tiles_across

    def tile_of(ref, lead, d):
        r = pl.multiple_of((d // tiles_across) * ROWS, ROWS)
        c = pl.multiple_of((d % tiles_across) * LANES, LANES)
        return ref.at[lead + (pl.ds(r, ROWS), pl.ds(c, LANES))]

    def peers(send):
        y, z = me // RING, lax.rem(me, RING)

        @pl.loop(0, n_mem // RING)
        def _(j):
            ahead = lax.rem(y + n_mem // RING - 1 - j, n_mem // RING) * RING
            for t in range(RING):
                step = RING // 2 + (t // 2 if t % 2 == 0 else -(t + 1) // 2)
                d = ahead + lax.rem(z + step, RING)
                if step > 0:
                    send(d)
                else:
                    pl.when(j < n_mem // RING - 1)(functools.partial(send, d))

    def fetch(s):
        return (
            pltpu.make_async_copy(prior.at[:, s], pin.at[s], in_sem.at[0, s]),
            pltpu.make_async_copy(vert.at[s], vin.at[s], in_sem.at[1, s]),
            pltpu.make_async_copy(horz.at[s], hin.at[s], in_sem.at[2, s]),
        )

    small = [
        pltpu.make_async_copy(a, b, obs_sem.at[i])
        for i, (a, b) in enumerate(
            (
                (diff_in, diff),
                (cells_in, cells),
                (slabs_in, slabs),
                (vals_in, vals),
                (errs_in, errs),
            )
        )
    ]
    for copy in small:
        copy.start()

    @pl.loop(0, n_slab)
    def _(s):
        for copy in fetch(s):
            copy.start()

    barrier = pltpu.get_barrier_semaphore()

    @pl.loop(1, n_mem)
    def _(i):
        pl.semaphore_signal(
            barrier, inc=1, device_id={"mem": lax.rem(me + i, n_mem)}, device_id_type=MESH
        )

    @pl.loop(1, n_lev)
    def _(i):
        pl.semaphore_signal(
            barrier, inc=1, device_id={"lev": lax.rem(lev + i, n_lev)}, device_id_type=MESH
        )

    col = lax.broadcasted_iota(jnp.int32, (grid_rows, grid_cols), 1)
    row = lax.broadcasted_iota(jnp.int32, (grid_rows, grid_cols), 0)

    def forecast(s):
        for copy in fetch(s):
            copy.wait()
        d = diff[s]
        v = 0.5 * vin[s]
        h = 0.5 * hin[s]
        coef[0] = d - v
        coef[1] = d + v
        coef[2] = d - h
        coef[3] = d + h
        centre = 1.0 - 4.0 * d

        @pl.loop(0, mem_dev)
        def _(p):
            f = pin[s, p]
            for _step in range(STEPS):
                east = jnp.where(col == grid_cols - 1, f, pltpu.roll(f, grid_cols - 1, 1))
                west = jnp.where(col == 0, f, pltpu.roll(f, 1, 1))
                north = jnp.where(row == grid_rows - 1, f, pltpu.roll(f, grid_rows - 1, 0))
                south = jnp.where(row == 0, f, pltpu.roll(f, 1, 0))
                f = (
                    centre * f
                    + (coef[0] * east + coef[1] * west)
                    + (coef[2] * north + coef[3] * south)
                )
            field[s, p] = f

    def send_blocks(s):
        for p in range(mem_dev):
            blocks[s, me, p] = field[
                s,
                p,
                pl.ds(pl.multiple_of(tile_row * ROWS, ROWS), ROWS),
                pl.ds(pl.multiple_of(tile_col * LANES, LANES), LANES),
            ]

        @peers
        def _(d):
            pltpu.make_async_remote_copy(
                src_ref=tile_of(field, (s, slice(None)), d),
                dst_ref=blocks.at[s, me],
                send_sem=out_send.at[s],
                recv_sem=out_recv.at[s],
                device_id={"mem": d},
                device_id_type=MESH,
            ).start()

    for copy in small:
        copy.wait()
    forecast(0)
    pl.semaphore_wait(barrier, n_mem - 1 + n_lev - 1)
    send_blocks(0)

    @pl.loop(1, EARLY)
    def _(s):
        forecast(s)
        send_blocks(s)

    @pl.loop(EARLY, n_slab)
    def _(s):
        forecast(s)

    lane512 = lax.broadcasted_iota(jnp.int32, (1, grid_cols), 1)

    @pl.loop(0, n_obs)
    def _(k):
        b, q = k // n_per, lax.rem(k, n_per)
        cell = cells[b, q]
        at_row, at_col = lax.shift_right_logical(cell, 9), jnp.bitwise_and(cell, NX - 1)
        off = slabs[b, q] - lev * n_slab
        inside = jnp.logical_and(off >= 0, off < n_slab)
        wanted = jnp.where(inside, at_col, -1)
        near = jnp.clip(off, 0, n_slab - 1)
        for p in range(mem_dev):
            line = field[near, p, pl.ds(at_row, 1), :]
            line = jnp.where(lane512 == wanted, line, 0.0)
            total = line[:, :LANES]
            for t in range(1, tiles_across):
                total = total + line[:, t * LANES : (t + 1) * LANES]
            picked[p, pl.ds(k, 1), :] = total
        place[0, pl.ds(k, 1), :] = jnp.full((1, LANES), at_row.astype(jnp.float32))
        place[1, pl.ds(k, 1), :] = jnp.full((1, LANES), at_col.astype(jnp.float32))

    sub32 = lax.broadcasted_iota(jnp.int32, (n_obs, LANES), 0)
    lane32 = lax.broadcasted_iota(jnp.int32, (n_obs, LANES), 1)
    share = jnp.zeros((1, LANES), jnp.float32)
    for p in range(mem_dev):
        column = jnp.sum(picked[p], axis=1, keepdims=True)
        share = share + jnp.sum(
            jnp.where(lane32 == sub32 + p * half, column, 0.0), axis=0, keepdims=True
        )
    msg[0] = share
    got_mem[me] = share

    @peers
    def _(d):
        pltpu.make_async_remote_copy(
            src_ref=msg.at[0],
            dst_ref=got_mem.at[me],
            send_sem=mem_send,
            recv_sem=mem_recv,
            device_id={"mem": d},
            device_id_type=MESH,
        ).start()

    @pl.loop(EARLY, MIDDLE)
    def _(s):
        send_blocks(s)

    cell_row = (
        tile_row * ROWS + lax.broadcasted_iota(jnp.int32, (ROWS, LANES), 0)
    ).astype(jnp.float32)
    cell_col = (
        tile_col * LANES + lax.broadcasted_iota(jnp.int32, (ROWS, LANES), 1)
    ).astype(jnp.float32)

    def lev_rows(copies):
        return got_lev.at[pl.ds(0, copies)]

    pltpu.make_async_copy(
        got_mem.at[pl.ds(0, n_mem - 1)], got_mem.at[pl.ds(0, n_mem - 1)], mem_recv
    ).wait()

    @pl.loop(0, n_mem)
    def _(i):
        got_lev[lev, pl.ds(i, 1), :] = got_mem[i]

    @pl.loop(1, n_lev)
    def _(i):
        pltpu.make_async_remote_copy(
            src_ref=got_lev.at[lev],
            dst_ref=got_lev.at[lev],
            send_sem=lev_send,
            recv_sem=lev_recv,
            device_id={"lev": lax.rem(lev + i, n_lev)},
            device_id_type=MESH,
        ).start()

    @pl.loop(MIDDLE, n_slab)
    def _(s):
        send_blocks(s)

    @pl.loop(0, n_obs)
    def _(k):
        b, q = k // n_per, lax.rem(k, n_per)
        cell = cells[b, q]
        r = lax.shift_right_logical(cell, 9).astype(jnp.float32)
        c = jnp.bitwise_and(cell, NX - 1).astype(jnp.float32)
        dr, dc = place[0] - r, place[1] - c
        obs_loc[k] = taper(jnp.sqrt(dr * dr + dc * dc))
        dr, dc = cell_row - r, cell_col - c
        cell_loc[k] = taper(jnp.sqrt(dr * dr + dc * dc))

    square[n_mem:, :] = jnp.zeros((LANES - n_mem, LANES), jnp.float32)
    pltpu.make_async_copy(lev_rows(n_lev - 1), lev_rows(n_lev - 1), lev_recv).wait()
    square[:n_mem, :] = jnp.sum(got_lev[...], axis=0)
    turned = square[...].T
    rows = turned[:n_obs]
    for p in range(1, mem_dev):
        rows = rows + pltpu.roll(turned[p * half : p * half + n_obs], p * half, 1)
    rows_mean = jnp.sum(rows, axis=1, keepdims=True) * (1.0 / members)
    used = lax.rem(lane32, half) < n_mem
    anom[...] = jnp.where(used, rows - rows_mean, 0.0)
    mean[...] = jnp.broadcast_to(rows_mean, (n_obs, LANES))
    lane1 = lax.broadcasted_iota(jnp.int32, (1, LANES), 1)

    @pl.loop(0, n_obs)
    def _(k):
        b, q = k // n_per, lax.rem(k, n_per)
        r, o = errs[b, q], vals[b, q]
        a = anom[pl.ds(k, 1), :]
        m = mean[pl.ds(k, 1), :]
        every = anom[...]
        g = jnp.sum(every * a, axis=1, keepdims=True)
        v = jnp.sum(a * a, axis=1, keepdims=True) * (1.0 / (members - 1)) + 1e-06
        v = jnp.broadcast_to(v, (1, LANES))
        inv = 1.0 / (v + r)
        less = jnp.sqrt(r * inv) - 1.0
        move = (m * r + o * v) * inv - m
        gain = 1.0 / ((members - 1) * v)
        c = obs_loc[k] * g * gain
        anom[...] = every + (c * less) * a
        mean[...] = mean[...] + c * move
        ys[pl.ds(k, 1), :] = a
        plan[pl.ds(n_obs + k, 1), :] = jnp.where(
            lane1 == 0, less, jnp.where(lane1 == 1, move, gain)
        )

    def product(a, b, axis=0):
        return lax.dot_general(
            a,
            b,
            (((1,), (axis,)), ((), ())),
            precision=lax.Precision.HIGHEST,
            preferred_element_type=jnp.float32,
        )

    y = ys[...]
    plan[:n_obs, :n_obs] = product(y, y, 1)
    square[:n_obs, :] = y
    square[n_obs:, :] = jnp.zeros((LANES - n_obs, LANES), jnp.float32)
    turned = square[...].T
    at = lax.broadcasted_iota(jnp.int32, (LANES, members * ROWS), 1) // ROWS
    lane_of = lax.rem(at, mem_dev) * half + at // mem_dev
    pick_in = (lane_of == lax.broadcasted_iota(jnp.int32, (LANES, members * ROWS), 0)).astype(
        jnp.float32
    )
    wide[...] = product(y, pick_in)
    pick_out = (
        lax.broadcasted_iota(jnp.int32, (LANES, n_obs * ROWS), 1) // ROWS
        == lax.broadcasted_iota(jnp.int32, (LANES, n_obs * ROWS), 0)
    ).astype(jnp.float32)
    tall[...] = product(turned, pick_out)

    def same_row(n):
        shape = (ROWS, n * ROWS)
        return lax.rem(lax.broadcasted_iota(jnp.int32, shape, 1), ROWS) == (
            lax.broadcasted_iota(jnp.int32, shape, 0)
        )

    @pl.loop(0, n_obs)
    def _(k):
        spread_in[pl.ds(pl.multiple_of(k * ROWS, ROWS), ROWS), :] = jnp.where(
            same_row(members), wide[pl.ds(k, 1), :], 0.0
        )

    @pl.loop(0, n_mem)
    def _(i):
        for p in range(mem_dev):
            at = pl.multiple_of((i * mem_dev + p) * ROWS, ROWS)
            spread_out[pl.ds(at, ROWS), :] = jnp.where(
                same_row(n_obs), tall[pl.ds(p * half + i, 1), :], 0.0
            )

    to_table = pltpu.make_async_copy(plan, table, plan_sem)
    to_table.start()
    to_table.wait()

    width = 8

    @pl.loop(0, n_slab)
    def _(s):
        pltpu.make_async_copy(
            blocks.at[s, pl.ds(0, n_mem - 1)], blocks.at[s, pl.ds(0, n_mem - 1)], out_recv.at[s]
        ).wait()

        x = blocks[s].reshape(members, ROWS, LANES)
        centre = jnp.sum(x, axis=0) * (1.0 / members)
        centred[...] = (x - centre).reshape(members * ROWS, LANES)
        cross[...] = product(spread_in[...], centred[...]).reshape(n_obs, ROWS, LANES)

        def solve(kb, base):
            k0 = kb * width

            def links(jb, acc):
                acc = list(acc)
                for f in range(width):
                    j = jb * width + f
                    x = push[j]
                    for e in range(width):
                        acc[e] = acc[e] + table[k0 + e, j] * x
                return tuple(acc)

            acc = tuple(cross[k0 + e] for e in range(width))
            acc = list(lax.fori_loop(0, kb, links, acc))
            for e in range(width):
                k = k0 + e
                w = (cell_loc[k] * table[n_obs + k, 2]) * acc[e]
                pushed = table[n_obs + k, 0] * w
                base = base + table[n_obs + k, 1] * w
                push[k] = pushed
                for f in range(e + 1, width):
                    acc[f] = acc[f] + table[k0 + f, k] * pushed
            return base

        base = lax.fori_loop(0, n_obs // width, solve, jnp.zeros((ROWS, LANES), jnp.float32))
        moved = product(spread_out[...], push[...].reshape(n_obs * ROWS, LANES))
        moved = moved.reshape(members, ROWS, LANES) + base
        blocks[s] = blocks[s] + moved.reshape(n_mem, mem_dev, ROWS, LANES)

        @peers
        def _(d):
            pltpu.make_async_remote_copy(
                src_ref=blocks.at[s, d],
                dst_ref=tile_of(out, (slice(None), s), me),
                send_sem=back_send,
                recv_sem=back_recv,
                device_id={"mem": d},
                device_id_type=MESH,
            ).start()

    def own_copy(s):
        return pltpu.make_async_copy(
            blocks.at[s, me], tile_of(out, (slice(None), s), me), own_sem.at[s]
        )

    @pl.loop(0, n_slab)
    def _(s):
        own_copy(s).start()

    others = blocks.at[:, pl.ds(0, n_mem - 1)]

    @pl.loop(0, n_slab)
    def _(s):
        sent = blocks.at[s, pl.ds(0, n_mem - 1)]
        pltpu.make_async_copy(sent, sent, out_send.at[s]).wait()
        own_copy(s).wait()

    pltpu.make_async_copy(lev_rows(n_lev - 1), lev_rows(n_lev - 1), lev_send).wait()
    pltpu.make_async_copy(
        got_mem.at[pl.ds(0, n_mem - 1)], got_mem.at[pl.ds(0, n_mem - 1)], mem_send
    ).wait()
    pltpu.make_async_copy(others, others, back_send).wait()
    pltpu.make_async_copy(others, others, back_recv).wait()


def body(*operands):
    prior, _, _, diff, cells, slabs, vals, errs = operands
    n_mem, n_lev = lax.axis_size("mem"), lax.axis_size("lev")
    mem_dev, n_slab, grid_rows, grid_cols = prior.shape
    n_obs = cells.size
    members = mem_dev * n_mem
    f32 = jnp.float32
    whole = pl.BlockSpec(memory_space=pl.ANY)
    dma = pltpu.SemaphoreType.DMA
    return pl.pallas_call(
        functools.partial(kernel, n_mem, n_lev),
        out_shape=jax.ShapeDtypeStruct(prior.shape, prior.dtype),
        in_specs=[whole] * 8,
        out_specs=whole,
        scratch_shapes=[
            pltpu.SMEM(diff.shape, diff.dtype),
            pltpu.SMEM(cells.shape, cells.dtype),
            pltpu.SMEM(slabs.shape, slabs.dtype),
            pltpu.SMEM(vals.shape, vals.dtype),
            pltpu.SMEM(errs.shape, errs.dtype),
            pltpu.VMEM((n_slab, mem_dev, grid_rows, grid_cols), f32),
            pltpu.VMEM((n_slab, grid_rows, grid_cols), f32),
            pltpu.VMEM((n_slab, grid_rows, grid_cols), f32),
            pltpu.VMEM((4, grid_rows, grid_cols), f32),
            pltpu.VMEM((n_slab, mem_dev, grid_rows, grid_cols), f32),
            pltpu.VMEM((n_slab, n_mem, mem_dev, ROWS, LANES), f32),
            pltpu.VMEM((n_lev, n_mem, LANES), f32),
            pltpu.VMEM((n_mem, 1, LANES), f32),
            pltpu.VMEM((1, 1, LANES), f32),
            pltpu.VMEM((mem_dev, n_obs, LANES), f32),
            pltpu.VMEM((LANES, LANES), f32),
            pltpu.VMEM((n_obs, LANES), f32),
            pltpu.VMEM((n_obs, LANES), f32),
            pltpu.VMEM((n_obs, n_obs, LANES), f32),
            pltpu.VMEM((2, n_obs, LANES), f32),
            pltpu.VMEM((2 * n_obs, LANES), f32),
            pltpu.SMEM((2 * n_obs, LANES), f32),
            pltpu.VMEM((n_obs, ROWS, LANES), f32),
            pltpu.VMEM((n_obs, LANES), f32),
            pltpu.VMEM((n_obs, members * ROWS), f32),
            pltpu.VMEM((LANES, n_obs * ROWS), f32),
            pltpu.VMEM((n_obs * ROWS, members * ROWS), f32),
            pltpu.VMEM((members * ROWS, n_obs * ROWS), f32),
            pltpu.VMEM((members * ROWS, LANES), f32),
            pltpu.VMEM((n_obs, ROWS, LANES), f32),
            pltpu.VMEM((n_obs, ROWS, LANES), f32),
            dma((3, n_slab)),
            dma((5,)),
            dma,
            dma,
            dma,
            dma,
            dma((n_slab,)),
            dma((n_slab,)),
            dma,
            dma,
            dma,
            dma((n_slab,)),
        ],
        compiler_params=pltpu.CompilerParams(
            collective_id=0, has_side_effects=True, vmem_limit_bytes=40 << 20
        ),
        name="filter_cycle",
    )(*(pltpu.with_memory_space_constraint(a, pltpu.HBM) for a in operands))


def solution(mesh):
    in_specs = (
        P("mem", "lev", None, None),
        P("lev", None, None),
        P("lev", None, None),
        P("lev"),
        P(),
        P(),
        P(),
        P(),
    )
    out_specs = P("mem", "lev", None, None)
    return jax.shard_map(body, mesh=mesh, in_specs=in_specs, out_specs=out_specs, check_vma=False)
```

```python
import functools

import jax
import jax.numpy as jnp
from jax import lax
from jax.experimental import pallas as pl
from jax.experimental.pallas import tpu as pltpu
from jax.sharding import PartitionSpec as P

NX = 512
STEPS = 2
LOC_HALF = 64
MESH = pl.DeviceIdType.MESH
ROWS, LANES = 8, 128
RING = 8
MIDDLE = 2
EARLY = 1


def taper(dist):
    scaled = dist * (1.0 / LOC_HALF)
    inner = (
        ((-0.25 * scaled + 0.5) * scaled + 0.625) * scaled - 5.0 / 3.0
    ) * scaled * scaled + 1.0
    safe = jnp.maximum(scaled, 1.0)
    outer = (
        ((((scaled * (1.0 / 12.0) - 0.5) * scaled + 0.625) * scaled + 5.0 / 3.0) * scaled - 5.0)
        * scaled
        + 4.0
        - 2.0 / (3.0 * safe)
    )
    return jnp.where(scaled <= 1.0, inner, jnp.where(scaled < 2.0, outer, 0.0))


def kernel(
    n_mem,
    n_lev,
    prior,
    vert,
    horz,
    diff_in,
    cells_in,
    slabs_in,
    vals_in,
    errs_in,
    out,
    diff,
    cells,
    slabs,
    vals,
    errs,
    pin,
    vin,
    hin,
    coef,
    field,
    blocks,
    got_lev,
    got_mem,
    msg,
    picked,
    square,
    anom,
    mean,
    obs_loc,
    place,
    plan,
    table,
    cell_loc,
    ys,
    wide,
    tall,
    spread_in,
    spread_out,
    centred,
    cross,
    push,
    in_sem,
    obs_sem,
    lev_send,
    lev_recv,
    mem_send,
    mem_recv,
    out_send,
    out_recv,
    back_send,
    back_recv,
    plan_sem,
    own_sem,
):
    mem_dev, n_slab, grid_rows, grid_cols = prior.shape
    n_batch, n_per = cells.shape
    n_obs = n_batch * n_per
    members = mem_dev * n_mem
    half = LANES // mem_dev
    tiles_across = grid_cols // LANES
    me = lax.axis_index("mem")
    lev = lax.axis_index("lev")
    tile_row, tile_col = me // tiles_across, me % tiles_across

    def tile_of(ref, lead, d):
        r = pl.multiple_of(lax.div(d, tiles_across) * ROWS, ROWS)
        c = pl.multiple_of(jnp.bitwise_and(d, tiles_across - 1) * LANES, LANES)
        return ref.at[lead + (pl.ds(r, ROWS), pl.ds(c, LANES))]

    barrier = pltpu.get_barrier_semaphore()

    @pl.loop(1, n_mem)
    def _(i):
        pl.semaphore_signal(
            barrier, inc=1, device_id={"mem": jnp.bitwise_and(me + i, n_mem - 1)}, device_id_type=MESH
        )

    @pl.loop(1, n_lev)
    def _(i):
        pl.semaphore_signal(
            barrier, inc=1, device_id={"lev": jnp.bitwise_and(lev + i, n_lev - 1)}, device_id_type=MESH
        )

    def peers(send):
        y, z = lax.div(me, RING), jnp.bitwise_and(me, RING - 1)

        @pl.loop(0, n_mem // RING)
        def _(j):
            ahead = jnp.bitwise_and(y - 1 - j, n_mem // RING - 1) * RING
            for t in range(RING):
                step = RING // 2 + (t // 2 if t % 2 == 0 else -(t + 1) // 2)
                d = ahead + jnp.bitwise_and(z + step, RING - 1)
                if step > 0:
                    send(d)
                else:
                    pl.when(j < n_mem // RING - 1)(functools.partial(send, d))

    def fetch(s):
        return (
            pltpu.make_async_copy(prior.at[:, s], pin.at[s], in_sem.at[0, s]),
            pltpu.make_async_copy(vert.at[s], vin.at[s], in_sem.at[1, s]),
            pltpu.make_async_copy(horz.at[s], hin.at[s], in_sem.at[2, s]),
        )

    small = [
        pltpu.make_async_copy(a, b, obs_sem.at[i])
        for i, (a, b) in enumerate(
            (
                (diff_in, diff),
                (cells_in, cells),
                (slabs_in, slabs),
                (vals_in, vals),
                (errs_in, errs),
            )
        )
    ]
    for copy in fetch(0):
        copy.start()
    for copy in small:
        copy.start()

    @pl.loop(1, n_slab)
    def _(s):
        for copy in fetch(s):
            copy.start()

    col = lax.broadcasted_iota(jnp.int32, (grid_rows, grid_cols), 1)
    row = lax.broadcasted_iota(jnp.int32, (grid_rows, grid_cols), 0)

    def forecast(s):
        for copy in fetch(s):
            copy.wait()
        d = diff[s]
        v = 0.5 * vin[s]
        h = 0.5 * hin[s]
        coef[0] = d - v
        coef[1] = d + v
        coef[2] = d - h
        coef[3] = d + h
        centre = 1.0 - 4.0 * d

        @pl.loop(0, mem_dev)
        def _(p):
            f = pin[s, p]
            for _step in range(STEPS):
                east = jnp.where(col == grid_cols - 1, f, pltpu.roll(f, grid_cols - 1, 1))
                west = jnp.where(col == 0, f, pltpu.roll(f, 1, 1))
                north = jnp.where(row == grid_rows - 1, f, pltpu.roll(f, grid_rows - 1, 0))
                south = jnp.where(row == 0, f, pltpu.roll(f, 1, 0))
                f = (
                    centre * f
                    + (coef[0] * east + coef[1] * west)
                    + (coef[2] * north + coef[3] * south)
                )
            field[s, p] = f

    def send_blocks(s):
        for p in range(mem_dev):
            blocks[s, me, p] = field[
                s,
                p,
                pl.ds(pl.multiple_of(tile_row * ROWS, ROWS), ROWS),
                pl.ds(pl.multiple_of(tile_col * LANES, LANES), LANES),
            ]

        @peers
        def _(d):
            pltpu.make_async_remote_copy(
                src_ref=tile_of(field, (s, slice(None)), d),
                dst_ref=blocks.at[s, me],
                send_sem=out_send.at[s],
                recv_sem=out_recv.at[s],
                device_id={"mem": d},
                device_id_type=MESH,
            ).start()

    for copy in small:
        copy.wait()
    forecast(0)
    pl.semaphore_wait(barrier, n_mem - 1 + n_lev - 1)
    send_blocks(0)

    @pl.loop(1, EARLY)
    def _(s):
        forecast(s)
        send_blocks(s)

    @pl.loop(EARLY, n_slab)
    def _(s):
        forecast(s)

    lane512 = lax.broadcasted_iota(jnp.int32, (1, grid_cols), 1)

    @pl.loop(0, n_obs)
    def _(k):
        b, q = k // n_per, lax.rem(k, n_per)
        cell = cells[b, q]
        at_row, at_col = lax.shift_right_logical(cell, 9), jnp.bitwise_and(cell, NX - 1)
        off = slabs[b, q] - lev * n_slab
        inside = jnp.logical_and(off >= 0, off < n_slab)
        wanted = jnp.where(inside, at_col, -1)
        near = jnp.clip(off, 0, n_slab - 1)
        for p in range(mem_dev):
            line = field[near, p, pl.ds(at_row, 1), :]
            line = jnp.where(lane512 == wanted, line, 0.0)
            total = line[:, :LANES]
            for t in range(1, tiles_across):
                total = total + line[:, t * LANES : (t + 1) * LANES]
            picked[p, pl.ds(k, 1), :] = total
        place[0, pl.ds(k, 1), :] = jnp.full((1, LANES), at_row.astype(jnp.float32))
        place[1, pl.ds(k, 1), :] = jnp.full((1, LANES), at_col.astype(jnp.float32))

    sub32 = lax.broadcasted_iota(jnp.int32, (n_obs, LANES), 0)
    lane32 = lax.broadcasted_iota(jnp.int32, (n_obs, LANES), 1)
    share = jnp.zeros((1, LANES), jnp.float32)
    for p in range(mem_dev):
        column = jnp.sum(picked[p], axis=1, keepdims=True)
        share = share + jnp.sum(
            jnp.where(lane32 == sub32 + p * half, column, 0.0), axis=0, keepdims=True
        )
    msg[0] = share
    got_mem[me] = share

    @peers
    def _(d):
        pltpu.make_async_remote_copy(
            src_ref=msg.at[0],
            dst_ref=got_mem.at[me],
            send_sem=mem_send,
            recv_sem=mem_recv,
            device_id={"mem": d},
            device_id_type=MESH,
        ).start()

    @pl.loop(EARLY, MIDDLE)
    def _(s):
        send_blocks(s)

    cell_row = (
        tile_row * ROWS + lax.broadcasted_iota(jnp.int32, (ROWS, LANES), 0)
    ).astype(jnp.float32)
    cell_col = (
        tile_col * LANES + lax.broadcasted_iota(jnp.int32, (ROWS, LANES), 1)
    ).astype(jnp.float32)

    def lev_rows(copies):
        return got_lev.at[pl.ds(0, copies)]

    pltpu.make_async_copy(
        got_mem.at[pl.ds(0, n_mem - 1)], got_mem.at[pl.ds(0, n_mem - 1)], mem_recv
    ).wait()

    @pl.loop(0, n_mem)
    def _(i):
        got_lev[lev, pl.ds(i, 1), :] = got_mem[i]

    @pl.loop(1, n_lev)
    def _(i):
        pltpu.make_async_remote_copy(
            src_ref=got_lev.at[lev],
            dst_ref=got_lev.at[lev],
            send_sem=lev_send,
            recv_sem=lev_recv,
            device_id={"lev": jnp.bitwise_and(lev + i, n_lev - 1)},
            device_id_type=MESH,
        ).start()

    @pl.loop(MIDDLE, n_slab)
    def _(s):
        send_blocks(s)

    @pl.loop(0, n_obs)
    def _(k):
        b, q = k // n_per, lax.rem(k, n_per)
        cell = cells[b, q]
        r = lax.shift_right_logical(cell, 9).astype(jnp.float32)
        c = jnp.bitwise_and(cell, NX - 1).astype(jnp.float32)
        dr, dc = place[0] - r, place[1] - c
        obs_loc[k] = taper(jnp.sqrt(dr * dr + dc * dc))
        dr, dc = cell_row - r, cell_col - c
        cell_loc[k] = taper(jnp.sqrt(dr * dr + dc * dc))

    square[n_mem:, :] = jnp.zeros((LANES - n_mem, LANES), jnp.float32)
    pltpu.make_async_copy(lev_rows(n_lev - 1), lev_rows(n_lev - 1), lev_recv).wait()
    square[:n_mem, :] = jnp.sum(got_lev[...], axis=0)
    turned = square[...].T
    rows = turned[:n_obs]
    for p in range(1, mem_dev):
        rows = rows + pltpu.roll(turned[p * half : p * half + n_obs], p * half, 1)
    rows_mean = jnp.sum(rows, axis=1, keepdims=True) * (1.0 / members)
    used = lax.rem(lane32, half) < n_mem
    anom[...] = jnp.where(used, rows - rows_mean, 0.0)
    mean[...] = jnp.broadcast_to(rows_mean, (n_obs, LANES))
    lane1 = lax.broadcasted_iota(jnp.int32, (1, LANES), 1)

    @pl.loop(0, n_obs)
    def _(k):
        b, q = k // n_per, lax.rem(k, n_per)
        r, o = errs[b, q], vals[b, q]
        a = anom[pl.ds(k, 1), :]
        m = mean[pl.ds(k, 1), :]
        every = anom[...]
        g = jnp.sum(every * a, axis=1, keepdims=True)
        v = jnp.sum(a * a, axis=1, keepdims=True) * (1.0 / (members - 1)) + 1e-06
        v = jnp.broadcast_to(v, (1, LANES))
        inv = 1.0 / (v + r)
        less = jnp.sqrt(r * inv) - 1.0
        move = (m * r + o * v) * inv - m
        gain = 1.0 / ((members - 1) * v)
        c = obs_loc[k] * g * gain
        anom[...] = every + (c * less) * a
        mean[...] = mean[...] + c * move
        ys[pl.ds(k, 1), :] = a
        plan[pl.ds(n_obs + k, 1), :] = jnp.where(
            lane1 == 0, less, jnp.where(lane1 == 1, move, gain)
        )

    def product(a, b, axis=0):
        return lax.dot_general(
            a,
            b,
            (((1,), (axis,)), ((), ())),
            precision=lax.Precision.HIGHEST,
            preferred_element_type=jnp.float32,
        )

    y = ys[...]
    plan[:n_obs, :n_obs] = product(y, y, 1)
    square[:n_obs, :] = y
    square[n_obs:, :] = jnp.zeros((LANES - n_obs, LANES), jnp.float32)
    turned = square[...].T
    at = lax.broadcasted_iota(jnp.int32, (LANES, members * ROWS), 1) // ROWS
    lane_of = lax.rem(at, mem_dev) * half + at // mem_dev
    pick_in = (lane_of == lax.broadcasted_iota(jnp.int32, (LANES, members * ROWS), 0)).astype(
        jnp.float32
    )
    wide[...] = product(y, pick_in)
    pick_out = (
        lax.broadcasted_iota(jnp.int32, (LANES, n_obs * ROWS), 1) // ROWS
        == lax.broadcasted_iota(jnp.int32, (LANES, n_obs * ROWS), 0)
    ).astype(jnp.float32)
    tall[...] = product(turned, pick_out)

    def same_row(n):
        shape = (ROWS, n * ROWS)
        return lax.rem(lax.broadcasted_iota(jnp.int32, shape, 1), ROWS) == (
            lax.broadcasted_iota(jnp.int32, shape, 0)
        )

    @pl.loop(0, n_obs)
    def _(k):
        spread_in[pl.ds(pl.multiple_of(k * ROWS, ROWS), ROWS), :] = jnp.where(
            same_row(members), wide[pl.ds(k, 1), :], 0.0
        )

    @pl.loop(0, n_mem)
    def _(i):
        for p in range(mem_dev):
            at = pl.multiple_of((i * mem_dev + p) * ROWS, ROWS)
            spread_out[pl.ds(at, ROWS), :] = jnp.where(
                same_row(n_obs), tall[pl.ds(p * half + i, 1), :], 0.0
            )

    to_table = pltpu.make_async_copy(plan, table, plan_sem)
    to_table.start()
    to_table.wait()

    width = 8

    @pl.loop(0, n_slab)
    def _(s):
        pltpu.make_async_copy(
            blocks.at[s, pl.ds(0, n_mem - 1)], blocks.at[s, pl.ds(0, n_mem - 1)], out_recv.at[s]
        ).wait()

        x = blocks[s].reshape(members, ROWS, LANES)
        centre = jnp.sum(x, axis=0) * (1.0 / members)
        centred[...] = (x - centre).reshape(members * ROWS, LANES)
        cross[...] = product(spread_in[...], centred[...]).reshape(n_obs, ROWS, LANES)

        def solve(kb, base):
            k0 = kb * width

            def links(jb, acc):
                acc = list(acc)
                for f in range(width):
                    j = jb * width + f
                    x = push[j]
                    for e in range(width):
                        acc[e] = acc[e] + table[k0 + e, j] * x
                return tuple(acc)

            acc = tuple(cross[k0 + e] for e in range(width))
            acc = list(lax.fori_loop(0, kb, links, acc))
            for e in range(width):
                k = k0 + e
                w = (cell_loc[k] * table[n_obs + k, 2]) * acc[e]
                pushed = table[n_obs + k, 0] * w
                base = base + table[n_obs + k, 1] * w
                push[k] = pushed
                for f in range(e + 1, width):
                    acc[f] = acc[f] + table[k0 + f, k] * pushed
            return base

        base = lax.fori_loop(0, n_obs // width, solve, jnp.zeros((ROWS, LANES), jnp.float32))
        moved = product(spread_out[...], push[...].reshape(n_obs * ROWS, LANES))
        moved = moved.reshape(members, ROWS, LANES) + base
        blocks[s] = blocks[s] + moved.reshape(n_mem, mem_dev, ROWS, LANES)

        @peers
        def _(d):
            pltpu.make_async_remote_copy(
                src_ref=blocks.at[s, d],
                dst_ref=tile_of(out, (slice(None), s), me),
                send_sem=back_send,
                recv_sem=back_recv,
                device_id={"mem": d},
                device_id_type=MESH,
            ).start()

    def own_copy(s):
        return pltpu.make_async_copy(
            blocks.at[s, me], tile_of(out, (slice(None), s), me), own_sem.at[s]
        )

    @pl.loop(0, n_slab)
    def _(s):
        own_copy(s).start()

    others = blocks.at[:, pl.ds(0, n_mem - 1)]

    @pl.loop(0, n_slab)
    def _(s):
        sent = blocks.at[s, pl.ds(0, n_mem - 1)]
        pltpu.make_async_copy(sent, sent, out_send.at[s]).wait()
        own_copy(s).wait()

    pltpu.make_async_copy(lev_rows(n_lev - 1), lev_rows(n_lev - 1), lev_send).wait()
    pltpu.make_async_copy(
        got_mem.at[pl.ds(0, n_mem - 1)], got_mem.at[pl.ds(0, n_mem - 1)], mem_send
    ).wait()
    pltpu.make_async_copy(others, others, back_send).wait()
    pltpu.make_async_copy(others, others, back_recv).wait()


def body(*operands):
    prior, _, _, diff, cells, slabs, vals, errs = operands
    n_mem, n_lev = lax.axis_size("mem"), lax.axis_size("lev")
    mem_dev, n_slab, grid_rows, grid_cols = prior.shape
    n_obs = cells.size
    members = mem_dev * n_mem
    f32 = jnp.float32
    whole = pl.BlockSpec(memory_space=pl.ANY)
    dma = pltpu.SemaphoreType.DMA
    return pl.pallas_call(
        functools.partial(kernel, n_mem, n_lev),
        out_shape=jax.ShapeDtypeStruct(prior.shape, prior.dtype),
        in_specs=[whole] * 8,
        out_specs=whole,
        scratch_shapes=[
            pltpu.SMEM(diff.shape, diff.dtype),
            pltpu.SMEM(cells.shape, cells.dtype),
            pltpu.SMEM(slabs.shape, slabs.dtype),
            pltpu.SMEM(vals.shape, vals.dtype),
            pltpu.SMEM(errs.shape, errs.dtype),
            pltpu.VMEM((n_slab, mem_dev, grid_rows, grid_cols), f32),
            pltpu.VMEM((n_slab, grid_rows, grid_cols), f32),
            pltpu.VMEM((n_slab, grid_rows, grid_cols), f32),
            pltpu.VMEM((4, grid_rows, grid_cols), f32),
            pltpu.VMEM((n_slab, mem_dev, grid_rows, grid_cols), f32),
            pltpu.VMEM((n_slab, n_mem, mem_dev, ROWS, LANES), f32),
            pltpu.VMEM((n_lev, n_mem, LANES), f32),
            pltpu.VMEM((n_mem, 1, LANES), f32),
            pltpu.VMEM((1, 1, LANES), f32),
            pltpu.VMEM((mem_dev, n_obs, LANES), f32),
            pltpu.VMEM((LANES, LANES), f32),
            pltpu.VMEM((n_obs, LANES), f32),
            pltpu.VMEM((n_obs, LANES), f32),
            pltpu.VMEM((n_obs, n_obs, LANES), f32),
            pltpu.VMEM((2, n_obs, LANES), f32),
            pltpu.VMEM((2 * n_obs, LANES), f32),
            pltpu.SMEM((2 * n_obs, LANES), f32),
            pltpu.VMEM((n_obs, ROWS, LANES), f32),
            pltpu.VMEM((n_obs, LANES), f32),
            pltpu.VMEM((n_obs, members * ROWS), f32),
            pltpu.VMEM((LANES, n_obs * ROWS), f32),
            pltpu.VMEM((n_obs * ROWS, members * ROWS), f32),
            pltpu.VMEM((members * ROWS, n_obs * ROWS), f32),
            pltpu.VMEM((members * ROWS, LANES), f32),
            pltpu.VMEM((n_obs, ROWS, LANES), f32),
            pltpu.VMEM((n_obs, ROWS, LANES), f32),
            dma((3, n_slab)),
            dma((5,)),
            dma,
            dma,
            dma,
            dma,
            dma((n_slab,)),
            dma((n_slab,)),
            dma,
            dma,
            dma,
            dma((n_slab,)),
        ],
        compiler_params=pltpu.CompilerParams(
            collective_id=0, has_side_effects=True, vmem_limit_bytes=40 << 20
        ),
        name="filter_cycle",
    )(*(pltpu.with_memory_space_constraint(a, pltpu.HBM) for a in operands))


def solution(mesh):
    in_specs = (
        P("mem", "lev", None, None),
        P("lev", None, None),
        P("lev", None, None),
        P("lev"),
        P(),
        P(),
        P(),
        P(),
    )
    out_specs = P("mem", "lev", None, None)
    return jax.shard_map(body, mesh=mesh, in_specs=in_specs, out_specs=out_specs, check_vma=False)
```

```python
import functools

import jax
import jax.numpy as jnp
from jax import lax
from jax.experimental import pallas as pl
from jax.experimental.pallas import tpu as pltpu
from jax.sharding import PartitionSpec as P

NX = 512
STEPS = 2
LOC_HALF = 64
MESH = pl.DeviceIdType.MESH
ROWS, LANES = 8, 128
RING = 8
MIDDLE = 2
EARLY = 1


def taper(dist):
    scaled = dist * (1.0 / LOC_HALF)
    inner = (
        ((-0.25 * scaled + 0.5) * scaled + 0.625) * scaled - 5.0 / 3.0
    ) * scaled * scaled + 1.0
    safe = jnp.maximum(scaled, 1.0)
    outer = (
        ((((scaled * (1.0 / 12.0) - 0.5) * scaled + 0.625) * scaled + 5.0 / 3.0) * scaled - 5.0)
        * scaled
        + 4.0
        - 2.0 / (3.0 * safe)
    )
    return jnp.where(scaled <= 1.0, inner, jnp.where(scaled < 2.0, outer, 0.0))


def kernel(
    n_mem,
    n_lev,
    prior,
    vert,
    horz,
    diff_in,
    cells_in,
    slabs_in,
    vals_in,
    errs_in,
    out,
    diff,
    cells,
    slabs,
    vals,
    errs,
    pin,
    vin,
    hin,
    coef,
    field,
    blocks,
    got_lev,
    got_mem,
    msg,
    picked,
    square,
    anom,
    mean,
    obs_loc,
    place,
    plan,
    table,
    cell_loc,
    ys,
    wide,
    tall,
    spread_in,
    spread_out,
    centred,
    cross,
    push,
    in_sem,
    obs_sem,
    lev_send,
    lev_recv,
    mem_send,
    mem_recv,
    out_send,
    out_recv,
    back_send,
    back_recv,
    plan_sem,
    own_sem,
):
    mem_dev, n_slab, grid_rows, grid_cols = prior.shape
    n_batch, n_per = cells.shape
    n_obs = n_batch * n_per
    members = mem_dev * n_mem
    half = LANES // mem_dev
    tiles_across = grid_cols // LANES
    me = lax.axis_index("mem")
    lev = lax.axis_index("lev")
    tile_row, tile_col = me // tiles_across, me % tiles_across

    def tile_of(ref, lead, d):
        r = pl.multiple_of(lax.div(d, tiles_across) * ROWS, ROWS)
        c = pl.multiple_of(jnp.bitwise_and(d, tiles_across - 1) * LANES, LANES)
        return ref.at[lead + (pl.ds(r, ROWS), pl.ds(c, LANES))]

    barrier = pltpu.get_barrier_semaphore()

    @pl.loop(1, n_mem)
    def _(i):
        pl.semaphore_signal(
            barrier, inc=1, device_id={"mem": jnp.bitwise_and(me + i, n_mem - 1)}, device_id_type=MESH
        )

    @pl.loop(1, n_lev)
    def _(i):
        pl.semaphore_signal(
            barrier, inc=1, device_id={"lev": jnp.bitwise_and(lev + i, n_lev - 1)}, device_id_type=MESH
        )

    def peers(send):
        y, z = lax.div(me, RING), jnp.bitwise_and(me, RING - 1)

        @pl.loop(0, n_mem // RING)
        def _(j):
            ahead = jnp.bitwise_and(y - 1 - j, n_mem // RING - 1) * RING
            for t in range(RING):
                step = RING // 2 + (t // 2 if t % 2 == 0 else -(t + 1) // 2)
                d = ahead + jnp.bitwise_and(z + step, RING - 1)
                if step > 0:
                    send(d)
                else:
                    pl.when(j < n_mem // RING - 1)(functools.partial(send, d))

    def fetch(s):
        return (
            pltpu.make_async_copy(prior.at[:, s], pin.at[s], in_sem.at[0, s]),
            pltpu.make_async_copy(vert.at[s], vin.at[s], in_sem.at[1, s]),
            pltpu.make_async_copy(horz.at[s], hin.at[s], in_sem.at[2, s]),
        )

    small = [
        pltpu.make_async_copy(a, b, obs_sem.at[i])
        for i, (a, b) in enumerate(
            (
                (diff_in, diff),
                (cells_in, cells),
                (slabs_in, slabs),
                (vals_in, vals),
                (errs_in, errs),
            )
        )
    ]
    for copy in fetch(0):
        copy.start()
    for copy in small:
        copy.start()

    @pl.loop(1, n_slab)
    def _(s):
        for copy in fetch(s):
            copy.start()

    col = lax.broadcasted_iota(jnp.int32, (grid_rows, grid_cols), 1)
    row = lax.broadcasted_iota(jnp.int32, (grid_rows, grid_cols), 0)

    def forecast(s):
        for copy in fetch(s):
            copy.wait()
        d = diff[s]
        v = 0.5 * vin[s]
        h = 0.5 * hin[s]
        coef[0] = d - v
        coef[1] = d + v
        coef[2] = d - h
        coef[3] = d + h
        centre = 1.0 - 4.0 * d

        @pl.loop(0, mem_dev)
        def _(p):
            f = pin[s, p]
            for _step in range(STEPS):
                east = jnp.where(col == grid_cols - 1, f, pltpu.roll(f, grid_cols - 1, 1))
                west = jnp.where(col == 0, f, pltpu.roll(f, 1, 1))
                north = jnp.where(row == grid_rows - 1, f, pltpu.roll(f, grid_rows - 1, 0))
                south = jnp.where(row == 0, f, pltpu.roll(f, 1, 0))
                f = (
                    centre * f
                    + (coef[0] * east + coef[1] * west)
                    + (coef[2] * north + coef[3] * south)
                )
            field[s, p] = f

    def send_blocks(s):
        for p in range(mem_dev):
            blocks[s, me, p] = field[
                s,
                p,
                pl.ds(pl.multiple_of(tile_row * ROWS, ROWS), ROWS),
                pl.ds(pl.multiple_of(tile_col * LANES, LANES), LANES),
            ]

        @peers
        def _(d):
            pltpu.make_async_remote_copy(
                src_ref=tile_of(field, (s, slice(None)), d),
                dst_ref=blocks.at[s, me],
                send_sem=out_send.at[s],
                recv_sem=out_recv.at[s],
                device_id={"mem": d},
                device_id_type=MESH,
            ).start()

    for copy in small:
        copy.wait()
    forecast(0)
    pl.semaphore_wait(barrier, n_mem - 1 + n_lev - 1)
    send_blocks(0)

    @pl.loop(1, EARLY)
    def _(s):
        forecast(s)
        send_blocks(s)

    @pl.loop(EARLY, n_slab)
    def _(s):
        forecast(s)

    lane512 = lax.broadcasted_iota(jnp.int32, (1, grid_cols), 1)

    @pl.loop(0, n_obs)
    def _(k):
        b, q = k // n_per, lax.rem(k, n_per)
        cell = cells[b, q]
        at_row, at_col = lax.shift_right_logical(cell, 9), jnp.bitwise_and(cell, NX - 1)
        off = slabs[b, q] - lev * n_slab
        inside = jnp.logical_and(off >= 0, off < n_slab)
        wanted = jnp.where(inside, at_col, -1)
        near = jnp.clip(off, 0, n_slab - 1)
        for p in range(mem_dev):
            line = field[near, p, pl.ds(at_row, 1), :]
            line = jnp.where(lane512 == wanted, line, 0.0)
            total = line[:, :LANES]
            for t in range(1, tiles_across):
                total = total + line[:, t * LANES : (t + 1) * LANES]
            picked[p, pl.ds(k, 1), :] = total
        place[0, pl.ds(k, 1), :] = jnp.full((1, LANES), at_row.astype(jnp.float32))
        place[1, pl.ds(k, 1), :] = jnp.full((1, LANES), at_col.astype(jnp.float32))

    sub32 = lax.broadcasted_iota(jnp.int32, (n_obs, LANES), 0)
    lane32 = lax.broadcasted_iota(jnp.int32, (n_obs, LANES), 1)
    share = jnp.zeros((1, LANES), jnp.float32)
    for p in range(mem_dev):
        column = jnp.sum(picked[p], axis=1, keepdims=True)
        share = share + jnp.sum(
            jnp.where(lane32 == sub32 + p * half, column, 0.0), axis=0, keepdims=True
        )
    msg[0] = share
    got_mem[me] = share

    @peers
    def _(d):
        pltpu.make_async_remote_copy(
            src_ref=msg.at[0],
            dst_ref=got_mem.at[me],
            send_sem=mem_send,
            recv_sem=mem_recv,
            device_id={"mem": d},
            device_id_type=MESH,
        ).start()

    @pl.loop(EARLY, MIDDLE)
    def _(s):
        send_blocks(s)

    cell_row = (
        tile_row * ROWS + lax.broadcasted_iota(jnp.int32, (ROWS, LANES), 0)
    ).astype(jnp.float32)
    cell_col = (
        tile_col * LANES + lax.broadcasted_iota(jnp.int32, (ROWS, LANES), 1)
    ).astype(jnp.float32)

    def lev_rows(copies):
        return got_lev.at[pl.ds(0, copies)]

    pltpu.make_async_copy(
        got_mem.at[pl.ds(0, n_mem - 1)], got_mem.at[pl.ds(0, n_mem - 1)], mem_recv
    ).wait()

    @pl.loop(0, n_mem)
    def _(i):
        got_lev[lev, pl.ds(i, 1), :] = got_mem[i]

    @pl.loop(1, n_lev)
    def _(i):
        pltpu.make_async_remote_copy(
            src_ref=got_lev.at[lev],
            dst_ref=got_lev.at[lev],
            send_sem=lev_send,
            recv_sem=lev_recv,
            device_id={"lev": jnp.bitwise_and(lev + i, n_lev - 1)},
            device_id_type=MESH,
        ).start()

    @pl.loop(MIDDLE, n_slab)
    def _(s):
        send_blocks(s)

    @pl.loop(0, n_obs)
    def _(k):
        b, q = k // n_per, lax.rem(k, n_per)
        cell = cells[b, q]
        r = lax.shift_right_logical(cell, 9).astype(jnp.float32)
        c = jnp.bitwise_and(cell, NX - 1).astype(jnp.float32)
        dr, dc = place[0] - r, place[1] - c
        obs_loc[k] = taper(jnp.sqrt(dr * dr + dc * dc))
        dr, dc = cell_row - r, cell_col - c
        cell_loc[k] = taper(jnp.sqrt(dr * dr + dc * dc))

    square[n_mem:, :] = jnp.zeros((LANES - n_mem, LANES), jnp.float32)
    pltpu.make_async_copy(lev_rows(n_lev - 1), lev_rows(n_lev - 1), lev_recv).wait()
    square[:n_mem, :] = jnp.sum(got_lev[...], axis=0)
    turned = square[...].T
    rows = turned[:n_obs]
    for p in range(1, mem_dev):
        rows = rows + pltpu.roll(turned[p * half : p * half + n_obs], p * half, 1)
    rows_mean = jnp.sum(rows, axis=1, keepdims=True) * (1.0 / members)
    used = lax.rem(lane32, half) < n_mem
    anom[...] = jnp.where(used, rows - rows_mean, 0.0)
    mean[...] = jnp.broadcast_to(rows_mean, (n_obs, LANES))
    lane1 = lax.broadcasted_iota(jnp.int32, (1, LANES), 1)

    @pl.loop(0, n_obs)
    def _(k):
        b, q = k // n_per, lax.rem(k, n_per)
        r, o = errs[b, q], vals[b, q]
        a = anom[pl.ds(k, 1), :]
        m = mean[pl.ds(k, 1), :]
        every = anom[...]
        g = jnp.sum(every * a, axis=1, keepdims=True)
        v = jnp.sum(a * a, axis=1, keepdims=True) * (1.0 / (members - 1)) + 1e-06
        v = jnp.broadcast_to(v, (1, LANES))
        inv = 1.0 / (v + r)
        less = jnp.sqrt(r * inv) - 1.0
        move = (m * r + o * v) * inv - m
        gain = 1.0 / ((members - 1) * v)
        c = obs_loc[k] * g * gain
        anom[...] = every + (c * less) * a
        mean[...] = mean[...] + c * move
        ys[pl.ds(k, 1), :] = a
        plan[pl.ds(n_obs + k, 1), :] = jnp.where(
            lane1 == 0, less, jnp.where(lane1 == 1, move, gain)
        )

    def product(a, b, axis=0):
        return lax.dot_general(
            a,
            b,
            (((1,), (axis,)), ((), ())),
            precision=lax.Precision.HIGHEST,
            preferred_element_type=jnp.float32,
        )

    y = ys[...]
    plan[:n_obs, :n_obs] = product(y, y, 1)
    square[:n_obs, :] = y
    square[n_obs:, :] = jnp.zeros((LANES - n_obs, LANES), jnp.float32)
    turned = square[...].T
    at = lax.broadcasted_iota(jnp.int32, (LANES, members * ROWS), 1) // ROWS
    lane_of = lax.rem(at, mem_dev) * half + at // mem_dev
    pick_in = (lane_of == lax.broadcasted_iota(jnp.int32, (LANES, members * ROWS), 0)).astype(
        jnp.float32
    )
    wide[...] = product(y, pick_in)
    pick_out = (
        lax.broadcasted_iota(jnp.int32, (LANES, n_obs * ROWS), 1) // ROWS
        == lax.broadcasted_iota(jnp.int32, (LANES, n_obs * ROWS), 0)
    ).astype(jnp.float32)
    tall[...] = product(turned, pick_out)

    def same_row(n):
        shape = (ROWS, n * ROWS)
        return lax.rem(lax.broadcasted_iota(jnp.int32, shape, 1), ROWS) == (
            lax.broadcasted_iota(jnp.int32, shape, 0)
        )

    @pl.loop(0, n_obs)
    def _(k):
        spread_in[pl.ds(pl.multiple_of(k * ROWS, ROWS), ROWS), :] = jnp.where(
            same_row(members), wide[pl.ds(k, 1), :], 0.0
        )

    @pl.loop(0, n_mem)
    def _(i):
        for p in range(mem_dev):
            at = pl.multiple_of((i * mem_dev + p) * ROWS, ROWS)
            spread_out[pl.ds(at, ROWS), :] = jnp.where(
                same_row(n_obs), tall[pl.ds(p * half + i, 1), :], 0.0
            )

    to_table = pltpu.make_async_copy(plan, table, plan_sem)
    to_table.start()
    to_table.wait()

    def planes(first, count, send):
        y, z = me // RING, lax.rem(me, RING)

        @pl.loop(0, n_mem // RING)
        def _(j):
            ahead = lax.rem(y + n_mem // RING - 1 - j, n_mem // RING) * RING
            for t in range(count):
                d = ahead + first + lax.rem(z + count // 2 + t, count)
                pl.when(d != me)(functools.partial(send, d))

    def send_back(s, d):
        pltpu.make_async_remote_copy(
            src_ref=blocks.at[s, d],
            dst_ref=tile_of(out, (slice(None), s), me),
            send_sem=back_send,
            recv_sem=back_recv,
            device_id={"mem": d},
            device_id_type=MESH,
        ).start()

    width = 8

    @pl.loop(0, n_slab)
    def _(s):
        pltpu.make_async_copy(
            blocks.at[s, pl.ds(0, n_mem - 1)], blocks.at[s, pl.ds(0, n_mem - 1)], out_recv.at[s]
        ).wait()

        x = blocks[s].reshape(members, ROWS, LANES)
        centre = jnp.sum(x, axis=0) * (1.0 / members)
        centred[...] = (x - centre).reshape(members * ROWS, LANES)
        cross[...] = product(spread_in[...], centred[...]).reshape(n_obs, ROWS, LANES)

        def solve(kb, base):
            k0 = kb * width

            def links(jb, acc):
                acc = list(acc)
                for f in range(width):
                    j = jb * width + f
                    x = push[j]
                    for e in range(width):
                        acc[e] = acc[e] + table[k0 + e, j] * x
                return tuple(acc)

            acc = tuple(cross[k0 + e] for e in range(width))
            acc = list(lax.fori_loop(0, kb, links, acc))
            for e in range(width):
                k = k0 + e
                w = (cell_loc[k] * table[n_obs + k, 2]) * acc[e]
                pushed = table[n_obs + k, 0] * w
                base = base + table[n_obs + k, 1] * w
                push[k] = pushed
                for f in range(e + 1, width):
                    acc[f] = acc[f] + table[k0 + f, k] * pushed
            return base

        base = lax.fori_loop(0, n_obs // width, solve, jnp.zeros((ROWS, LANES), jnp.float32))
        moved = product(spread_out[...], push[...].reshape(n_obs * ROWS, LANES))
        moved = moved.reshape(members, ROWS, LANES) + base
        blocks[s] = blocks[s] + moved.reshape(n_mem, mem_dev, ROWS, LANES)

        planes(0, 1, functools.partial(send_back, s))

        @pl.when(jnp.logical_or(s < 4, jnp.bitwise_and(me, RING - 1) < 1))
        def _():
            planes(1, RING - 1, functools.partial(send_back, s))

    @pl.loop(4, n_slab)
    def _(s):
        @pl.when(jnp.bitwise_and(me, RING - 1) >= 1)
        def _():
            planes(1, 1, functools.partial(send_back, s))

        @pl.when(jnp.logical_and(jnp.bitwise_and(me, RING - 1) >= 1, jnp.bitwise_and(me, RING - 1) < 2))
        def _():
            planes(2, RING - 2, functools.partial(send_back, s))

    @pl.when(jnp.bitwise_and(me, RING - 1) >= 2)
    def _():
        @pl.loop(4, n_slab)
        def _(s):
            planes(2, RING - 2, functools.partial(send_back, s))

    def own_copy(s):
        return pltpu.make_async_copy(
            blocks.at[s, me], tile_of(out, (slice(None), s), me), own_sem.at[s]
        )

    @pl.loop(0, n_slab)
    def _(s):
        own_copy(s).start()

    others = blocks.at[:, pl.ds(0, n_mem - 1)]

    @pl.loop(0, n_slab)
    def _(s):
        sent = blocks.at[s, pl.ds(0, n_mem - 1)]
        pltpu.make_async_copy(sent, sent, out_send.at[s]).wait()
        own_copy(s).wait()

    pltpu.make_async_copy(lev_rows(n_lev - 1), lev_rows(n_lev - 1), lev_send).wait()
    pltpu.make_async_copy(
        got_mem.at[pl.ds(0, n_mem - 1)], got_mem.at[pl.ds(0, n_mem - 1)], mem_send
    ).wait()
    pltpu.make_async_copy(others, others, back_send).wait()
    pltpu.make_async_copy(others, others, back_recv).wait()


def body(*operands):
    prior, _, _, diff, cells, slabs, vals, errs = operands
    n_mem, n_lev = lax.axis_size("mem"), lax.axis_size("lev")
    mem_dev, n_slab, grid_rows, grid_cols = prior.shape
    n_obs = cells.size
    members = mem_dev * n_mem
    f32 = jnp.float32
    whole = pl.BlockSpec(memory_space=pl.ANY)
    dma = pltpu.SemaphoreType.DMA
    return pl.pallas_call(
        functools.partial(kernel, n_mem, n_lev),
        out_shape=jax.ShapeDtypeStruct(prior.shape, prior.dtype),
        in_specs=[whole] * 8,
        out_specs=whole,
        scratch_shapes=[
            pltpu.SMEM(diff.shape, diff.dtype),
            pltpu.SMEM(cells.shape, cells.dtype),
            pltpu.SMEM(slabs.shape, slabs.dtype),
            pltpu.SMEM(vals.shape, vals.dtype),
            pltpu.SMEM(errs.shape, errs.dtype),
            pltpu.VMEM((n_slab, mem_dev, grid_rows, grid_cols), f32),
            pltpu.VMEM((n_slab, grid_rows, grid_cols), f32),
            pltpu.VMEM((n_slab, grid_rows, grid_cols), f32),
            pltpu.VMEM((4, grid_rows, grid_cols), f32),
            pltpu.VMEM((n_slab, mem_dev, grid_rows, grid_cols), f32),
            pltpu.VMEM((n_slab, n_mem, mem_dev, ROWS, LANES), f32),
            pltpu.VMEM((n_lev, n_mem, LANES), f32),
            pltpu.VMEM((n_mem, 1, LANES), f32),
            pltpu.VMEM((1, 1, LANES), f32),
            pltpu.VMEM((mem_dev, n_obs, LANES), f32),
            pltpu.VMEM((LANES, LANES), f32),
            pltpu.VMEM((n_obs, LANES), f32),
            pltpu.VMEM((n_obs, LANES), f32),
            pltpu.VMEM((n_obs, n_obs, LANES), f32),
            pltpu.VMEM((2, n_obs, LANES), f32),
            pltpu.VMEM((2 * n_obs, LANES), f32),
            pltpu.SMEM((2 * n_obs, LANES), f32),
            pltpu.VMEM((n_obs, ROWS, LANES), f32),
            pltpu.VMEM((n_obs, LANES), f32),
            pltpu.VMEM((n_obs, members * ROWS), f32),
            pltpu.VMEM((LANES, n_obs * ROWS), f32),
            pltpu.VMEM((n_obs * ROWS, members * ROWS), f32),
            pltpu.VMEM((members * ROWS, n_obs * ROWS), f32),
            pltpu.VMEM((members * ROWS, LANES), f32),
            pltpu.VMEM((n_obs, ROWS, LANES), f32),
            pltpu.VMEM((n_obs, ROWS, LANES), f32),
            dma((3, n_slab)),
            dma((5,)),
            dma,
            dma,
            dma,
            dma,
            dma((n_slab,)),
            dma((n_slab,)),
            dma,
            dma,
            dma,
            dma((n_slab,)),
        ],
        compiler_params=pltpu.CompilerParams(
            collective_id=0, has_side_effects=True, vmem_limit_bytes=40 << 20
        ),
        name="filter_cycle",
    )(*(pltpu.with_memory_space_constraint(a, pltpu.HBM) for a in operands))


def solution(mesh):
    in_specs = (
        P("mem", "lev", None, None),
        P("lev", None, None),
        P("lev", None, None),
        P("lev"),
        P(),
        P(),
        P(),
        P(),
    )
    out_specs = P("mem", "lev", None, None)
    return jax.shard_map(body, mesh=mesh, in_specs=in_specs, out_specs=out_specs, check_vma=False)
```
